32 devices in a mesh: leaf: 4 (over z), row: 8 (over y, x, core).
Axes of the slice: x: 2, y: 2, z: 4, core: 2. Of those that a mesh axis runs over, the one named last changes fastest.
Arguments:
- sep_inverse: bfloat16 [4, 6144, 6144], P('leaf', 'row'), may hold values from -8 to 8, as said below
- rhs_block: bfloat16 [4, 6144, 512], P('leaf', 'row'), may hold values from -6 to 6
- coupling: bfloat16 [4, 4096, 6144], P('leaf', 'row'), may hold values from -0.078125 to 0.078125
- ancestor_rows: int32 [4, 4096], P('leaf', 'row'), may hold values from 0 to 4095, as said below
- ancestor_rhs: float32 [4096, 512], P('row', 'leaf'), may hold values from -12 to 12
Outputs:
- solution: bfloat16 [4, 6144, 512], P('leaf', 'row')
- ancestor_out: float32 [4096, 512], P('row', 'leaf')
The draws below stay inside these ranges and needn't reach their ends.
Inputs may be any that keep to these rules, and one draw needn't show every extreme that they name: Each block sep_inverse[g] is exactly symmetric. For each subtree, ancestor_rows is a one-to-one map of the 4096 coupling rows onto the ancestor rows that keeps every aligned block of 512 rows within itself.
All inputs are finite; a program needn't handle non-finite values.
Results may differ from the reference program's by a relative error of at most 0.014.
Values may be sent and summed in bfloat16 or wider, within the bound.
No kernel may reach another device: no remote copies, remote signals or barrier semaphores. Data moves between devices by JAX's collectives and lax.ppermute only.
A program may use at most 64 MiB of HBM per device.

```python
import math
import jax
import jax.numpy as jnp
from jax import lax

S = 6144
A = 4096
NRHS = 512
LEAVES = 4
ANC_DEV = 512
N_ROW = 8


def draw_sep_inverse(key, part):

    def one_leaf(leaf_key):
        key_raw, key_diag = jax.random.split(leaf_key, 2)
        spread = 0.9 / math.sqrt(S)
        raw = jax.random.uniform(key_raw, (S, S), jnp.float32, -spread, spread)
        matrix = (raw + raw.T) / math.sqrt(2.0)
        diag_values = jnp.exp(jax.random.uniform(key_diag, (S,), jnp.float32, math.log(0.5), math.log(2.0)))
        matrix = matrix + jnp.diag(diag_values)
        return matrix.astype(jnp.bfloat16)
    return lax.map(one_leaf, jax.random.split(jax.random.fold_in(key, 11), LEAVES))


def draw_ancestor_rows(key, part):
    keys = jax.random.split(jax.random.fold_in(key, 23), LEAVES * N_ROW)

    def block_perm(block_key):
        return jax.random.permutation(block_key, ANC_DEV).astype(jnp.int32)
    perms = jax.vmap(block_perm)(keys)
    offsets = jnp.arange(LEAVES * N_ROW, dtype=jnp.int32) % N_ROW * ANC_DEV
    return (perms + offsets[:, None]).reshape(LEAVES, A).astype(jnp.int32)


def steps_of(stream_key, shape, pieces, least, top_value):
    loudness = 1.0
    for position, blocks in pieces:
        draws = jax.random.uniform(jax.random.fold_in(jax.random.fold_in(stream_key, 6), position), (blocks,), jnp.float32, least / len(pieces), top_value / len(pieces))
        loudness = loudness * jnp.repeat(jnp.exp(draws), shape[position] // blocks).reshape((-1,) + (1,) * (len(shape) - 1 - position))
    return loudness


def scatter_about(own_key, shape, width, most, pieces=(), held_as=jnp.bfloat16):
    entries = width * jax.random.normal(own_key, shape, jnp.float32)
    if pieces:
        entries = entries * steps_of(own_key, shape, pieces, -0.22, 0.18)
    return jnp.clip(entries, -most, most).astype(held_as)


def setup_inputs(seed: int = 0) -> dict:
    arg_keys = jax.random.split(jax.random.key(seed), 6)
    sep_inverse = draw_sep_inverse(jax.random.fold_in(arg_keys[5], 71), 0)
    rhs_block = scatter_about(arg_keys[1], (LEAVES, S, NRHS), 1.0, 6.0, ((0, 4), (1, 8)))
    coupling = scatter_about(arg_keys[2], (LEAVES, A, S), S ** -0.5, 0.078125, ((0, 4), (1, 8)))
    ancestor_rows = draw_ancestor_rows(jax.random.fold_in(arg_keys[5], 71), 0)
    ancestor_rhs = scatter_about(arg_keys[4], (A, NRHS), 2.0, 12.0, ((0, 8), (1, 4)), jnp.float32)
    return {"sep_inverse": sep_inverse, "rhs_block": rhs_block, "coupling": coupling, "ancestor_rows": ancestor_rows, "ancestor_rhs": ancestor_rhs}


def reference(sep_inverse, rhs_block, coupling, ancestor_rows, ancestor_rhs):
    block_rows = S // N_ROW

    def one_subtree(running, items):
        inverse, rhs_part, couple, targets = items

        def add_block(total, block_idx):
            start = (block_idx * block_rows).astype(jnp.int32)
            columns = lax.dynamic_slice_in_dim(inverse, start, block_rows, 1)
            segment = lax.dynamic_slice_in_dim(rhs_part, start, block_rows, 0)
            partial_value = jnp.dot(columns, segment, preferred_element_type=jnp.float32).astype(jnp.bfloat16)
            return total + partial_value.astype(jnp.float32), None

        total0 = jnp.zeros((S, NRHS), jnp.float32)
        summed, _ = lax.scan(add_block, total0, jnp.arange(N_ROW, dtype=jnp.int32))
        solved = summed.astype(jnp.bfloat16)
        coupled = jnp.dot(couple, solved, preferred_element_type=jnp.float32)
        running = running.at[targets.astype(jnp.int32)].add(coupled)
        return running, solved

    start_sum = jnp.zeros((A, NRHS), jnp.float32)
    gathered_sum, solution = lax.scan(one_subtree, start_sum, (sep_inverse, rhs_block, coupling, ancestor_rows))
    return solution, ancestor_rhs - gathered_sum
```

```python
import functools

import jax
import jax.numpy as jnp
from jax import lax
from jax.experimental import pallas as pl
from jax.experimental.pallas import tpu as pltpu
from jax.sharding import PartitionSpec as P

VMEM = pl.BlockSpec(memory_space=pltpu.VMEM)
F32 = jnp.float32
BF16 = jnp.bfloat16


def pick_kernel(order, src, out, sem):
    n, _, width = out.shape

    def copy(j):
        start = pl.multiple_of(order[j] * width, 128)
        return pltpu.make_async_copy(src.at[:, pl.ds(start, width)], out.at[j], sem.at[j])

    for j in range(n):
        copy(j).start()
    for j in range(n):
        copy(j).wait()


def column_block(src, start, width):
    return lax.dynamic_slice_in_dim(src, start * width, width, 1)


def pick(src, order, width):
    n = order.shape[0]
    if width % 128:
        return jnp.stack([column_block(src, order[j], width) for j in range(n)])
    return pl.pallas_call(
        pick_kernel,
        out_shape=jax.ShapeDtypeStruct((n, src.shape[0], width), src.dtype),
        in_specs=[pl.BlockSpec(memory_space=pltpu.SMEM), pl.BlockSpec(memory_space=pl.ANY)],
        out_specs=VMEM,
        scratch_shapes=[pltpu.SemaphoreType.DMA((n,))],
        compiler_params=pltpu.CompilerParams(vmem_limit_bytes=8 << 20),
        name="pick",
    )(order, src)


def select_kernel(order, places, src, out):
    rows = out.shape[1]
    hot = lax.broadcasted_iota(jnp.int32, (rows, rows), 0) == places[...]
    hot = jnp.where(hot, 1.0, 0.0).astype(BF16)
    out[0] = jnp.dot(hot, src[...], preferred_element_type=F32).astype(BF16)


def select_rows(src, places, order, width):
    rows = src.shape[0]
    n = order.shape[0]
    if width % 128:
        hot = (lax.broadcasted_iota(jnp.int32, (rows, rows), 0) == places).astype(src.dtype)
        return jnp.stack([hot @ column_block(src, order[j], width) for j in range(n)])
    return pl.pallas_call(
        select_kernel,
        grid_spec=pltpu.PrefetchScalarGridSpec(
            num_scalar_prefetch=1,
            grid=(n,),
            in_specs=[
                pl.BlockSpec((1, rows), lambda j, order: (0, 0)),
                pl.BlockSpec((rows, width), lambda j, order: (0, order[j])),
            ],
            out_specs=pl.BlockSpec((1, rows, width), lambda j, order: (j, 0, 0)),
        ),
        out_shape=jax.ShapeDtypeStruct((n, rows, width), src.dtype),
        compiler_params=pltpu.CompilerParams(vmem_limit_bytes=10 << 20),
        name="select_rows",
    )(order, places, src)


def partial_kernel(n, keep, swap, *refs):
    pieces, (own, other) = refs[:n], refs[n:]
    own[...] = sum(
        jnp.dot(keep[j], pieces[j][...], preferred_element_type=F32) for j in range(n)
    )
    other[...] = sum(
        jnp.dot(swap[j], pieces[j][...], preferred_element_type=F32) for j in range(n)
    ).astype(BF16)


def partials(keep, swap, pieces):
    n, rows, _ = keep.shape
    width = pieces[0].shape[1]
    return pl.pallas_call(
        functools.partial(partial_kernel, n),
        out_shape=(
            jax.ShapeDtypeStruct((rows, width), F32),
            jax.ShapeDtypeStruct((rows, width), BF16),
        ),
        in_specs=[VMEM] * (2 + n),
        out_specs=(VMEM, VMEM),
        compiler_params=pltpu.CompilerParams(vmem_limit_bytes=12 << 20),
        name="partials",
    )(keep, swap, *pieces)


def on_device(sep_inverse, rhs_block, coupling, ancestor_rows, ancestor_rhs):
    inverse, rhs, couple = sep_inverse[0], rhs_block[0], coupling[0]
    leaves, n_row = lax.axis_size("leaf"), lax.axis_size("row")
    leaf, me = lax.axis_index("leaf"), lax.axis_index("row")
    core = me & 1
    rows = inverse.shape[0]
    anc = couple.shape[0]
    width = rhs.shape[1]
    narrow = width // leaves
    dims = [1 << b for b in range(1, n_row.bit_length() - 1)]
    routes = (dims, dims[::-1])
    masks = ([0], [0])
    for step in range(len(dims)):
        for k in (0, 1):
            masks[k].extend([m ^ routes[k][step] for m in masks[k]])

    def hop(x, step):
        return lax.ppermute(x, "row", [(i, i ^ routes[i & 1][step]) for i in range(n_row)])

    def partner(x):
        return lax.ppermute(x, "row", [(i, i ^ 1) for i in range(n_row)])

    def gather(x):
        pieces = [x]
        for step in range(len(dims)):
            pieces = pieces + [hop(p, step) for p in pieces]
        return pieces

    mask = jnp.where(core == 0, jnp.array(masks[0], jnp.int32), jnp.array(masks[1], jnp.int32))
    mask_other = jnp.where(core == 0, jnp.array(masks[1], jnp.int32), jnp.array(masks[0], jnp.int32))
    keep_order = me ^ mask
    send_order = (me ^ 1) ^ mask_other

    edge = leaves // 4
    inner = (leaf >= edge) & (leaf < leaves - edge)
    cut = edge * narrow

    def outer_cols(x):
        return jnp.concatenate([x[:, :cut], x[:, width - cut :]], axis=1)

    def inner_cols(x):
        return x[:, cut : width - cut]

    chunks = (
        (outer_cols(rhs), [j for j in range(leaves) if j < edge or j >= leaves - edge]),
        (inner_cols(rhs), [j for j in range(leaves) if edge <= j < leaves - edge]),
    )
    gathered = [gather(x) for x, _ in chunks]

    a_keep = pick(inverse, keep_order, rows)
    a_swap = partner(pick(inverse, send_order, rows))
    places = (ancestor_rows - me * anc).astype(jnp.int32)
    c_keep = select_rows(couple, places, keep_order, rows)
    c_swap = partner(select_rows(couple, places, send_order, rows))

    solved = []
    for pieces in gathered:
        own, other = partials(a_keep, a_swap, pieces)
        solved.append((own + partner(other).astype(F32)).astype(BF16))

    shares = []
    for (_, dests), y in zip(chunks, solved):
        own, other = partials(c_keep, c_swap, gather(y))
        q = own + partner(other).astype(F32)

        def piece(target):
            place = sum(jnp.where(target == j, i, 0) for i, j in enumerate(dests))
            return lax.dynamic_slice_in_dim(q, place * narrow, narrow, 1)

        total = piece(leaf)
        for d in range(1, leaves):
            got = lax.ppermute(
                piece(leaf ^ d).astype(BF16), "leaf", [(j ^ d, j) for j in dests]
            )
            total = total + got.astype(F32)
        shares.append(total)

    out = ancestor_rhs - jnp.where(inner, shares[1], shares[0])
    y_outer, y_inner = solved
    solution = jnp.concatenate([y_outer[:, :cut], y_inner, y_outer[:, cut:]], axis=1)
    return (solution[None], out)


def solution(mesh):
    return jax.shard_map(
        on_device,
        mesh=mesh,
        in_specs=(
            P("leaf", "row", None),
            P("leaf", "row", None),
            P("leaf", "row", None),
            P("leaf", "row"),
            P("row", "leaf"),
        ),
        out_specs=(P("leaf", "row", None), P("row", "leaf")),
        check_vma=False,
    )
```

```python
import functools

import jax
import jax.numpy as jnp
from jax import lax
from jax.experimental import pallas as pl
from jax.experimental.pallas import tpu as pltpu
from jax.sharding import PartitionSpec as P

VMEM = pl.BlockSpec(memory_space=pltpu.VMEM)
F32 = jnp.float32
BF16 = jnp.bfloat16


def pick_kernel(n, order, src, out, sem):
    width = out.shape[1] // n

    def copy(j):
        start = pl.multiple_of(order[j] * width, 128)
        return pltpu.make_async_copy(
            src.at[:, pl.ds(start, width)], out.at[:, pl.ds(j * width, width)], sem.at[j]
        )

    for j in range(n):
        copy(j).start()
    for j in range(n):
        copy(j).wait()


def column_block(src, start, width):
    return lax.dynamic_slice_in_dim(src, start * width, width, 1)


def pick(src, order, width):
    n = order.shape[0]
    if width % 128:
        return jnp.concatenate([column_block(src, order[j], width) for j in range(n)], axis=1)
    return pl.pallas_call(
        functools.partial(pick_kernel, n),
        out_shape=jax.ShapeDtypeStruct((src.shape[0], n * width), src.dtype),
        in_specs=[pl.BlockSpec(memory_space=pltpu.SMEM), pl.BlockSpec(memory_space=pltpu.HBM)],
        out_specs=VMEM,
        scratch_shapes=[pltpu.SemaphoreType.DMA((n,))],
        compiler_params=pltpu.CompilerParams(vmem_limit_bytes=8 << 20),
        name="pick",
    )(order, pltpu.with_memory_space_constraint(src, pltpu.HBM))


def select_kernel(n, order, places, src, out, buf, sem):
    rows, width = buf.shape[1:]

    def copy(j):
        start = pl.multiple_of(order[j] * width, 128)
        return pltpu.make_async_copy(src.at[:, pl.ds(start, width)], buf.at[j], sem.at[j])

    for j in range(n):
        copy(j).start()
    hot = lax.broadcasted_iota(jnp.int32, (rows, rows), 0) == places[...]
    hot = jnp.where(hot, 1.0, 0.0).astype(BF16)
    for j in range(n):
        copy(j).wait()
        out[:, j * width : (j + 1) * width] = jnp.dot(
            hot, buf[j], preferred_element_type=F32
        ).astype(BF16)


def select_rows(src, places, order, width):
    rows = src.shape[0]
    n = order.shape[0]
    if width % 128:
        hot = (lax.broadcasted_iota(jnp.int32, (rows, rows), 0) == places).astype(src.dtype)
        return hot @ pick(src, order, width)
    return pl.pallas_call(
        functools.partial(select_kernel, n),
        out_shape=jax.ShapeDtypeStruct((rows, n * width), src.dtype),
        in_specs=[
            pl.BlockSpec(memory_space=pltpu.SMEM),
            VMEM,
            pl.BlockSpec(memory_space=pltpu.HBM),
        ],
        out_specs=VMEM,
        scratch_shapes=[
            pltpu.VMEM((n, rows, width), src.dtype),
            pltpu.SemaphoreType.DMA((n,)),
        ],
        compiler_params=pltpu.CompilerParams(vmem_limit_bytes=12 << 20),
        name="select_rows",
    )(order, places, pltpu.with_memory_space_constraint(src, pltpu.HBM))


def partial_kernel(n, keep, swap, *refs):
    pieces, (own, other, joined) = refs[:n], refs[n:]
    depth = pieces[0].shape[0]
    for j in range(n):
        joined[j * depth : (j + 1) * depth, :] = pieces[j][...]
    other[...] = jnp.dot(swap[...], joined[...], preferred_element_type=F32).astype(BF16)
    own[...] = jnp.dot(keep[...], joined[...], preferred_element_type=F32)


def partials(keep, swap, pieces):
    n = len(pieces)
    rows, depth = keep.shape
    width = pieces[0].shape[1]
    return pl.pallas_call(
        functools.partial(partial_kernel, n),
        out_shape=(
            jax.ShapeDtypeStruct((rows, width), F32),
            jax.ShapeDtypeStruct((rows, width), BF16),
        ),
        in_specs=[VMEM] * (2 + n),
        out_specs=(VMEM, VMEM),
        scratch_shapes=[pltpu.VMEM((depth, width), BF16)],
        compiler_params=pltpu.CompilerParams(vmem_limit_bytes=12 << 20),
        name="partials",
    )(keep, swap, *pieces)


def on_device(sep_inverse, rhs_block, coupling, ancestor_rows, ancestor_rhs):
    inverse, rhs, couple = sep_inverse[0], rhs_block[0], coupling[0]
    leaves, n_row = lax.axis_size("leaf"), lax.axis_size("row")
    leaf, me = lax.axis_index("leaf"), lax.axis_index("row")
    core = me & 1
    rows = inverse.shape[0]
    anc = couple.shape[0]
    width = rhs.shape[1]
    narrow = width // leaves
    dims = [1 << b for b in range(1, n_row.bit_length() - 1)]
    routes = (dims, dims[::-1])
    masks = ([0], [0])
    for step in range(len(dims)):
        for k in (0, 1):
            masks[k].extend([m ^ routes[k][step] for m in masks[k]])

    def partner(x):
        return lax.ppermute(x, "row", [(i, i ^ 1) for i in range(n_row)])

    def gather(x):
        pieces = [x]
        for step in range(len(dims)):
            pairs = [(i, i ^ routes[i & 1][step]) for i in range(n_row)]
            for p in range(len(pieces)):
                pieces.append(lax.ppermute(pieces[p], "row", pairs))
        return pieces

    mask = jnp.where(core == 0, jnp.array(masks[0], jnp.int32), jnp.array(masks[1], jnp.int32))
    mask_other = jnp.where(core == 0, jnp.array(masks[1], jnp.int32), jnp.array(masks[0], jnp.int32))
    keep_order = me ^ mask
    send_order = (me ^ 1) ^ mask_other

    edge = leaves // 4
    inner = (leaf >= edge) & (leaf < leaves - edge)
    cut = edge * narrow

    def outer_cols(x):
        return jnp.concatenate([x[:, :cut], x[:, width - cut :]], axis=1)

    def inner_cols(x):
        return x[:, cut : width - cut]

    chunks = (
        (outer_cols(rhs), [j for j in range(leaves) if j < edge or j >= leaves - edge]),
        (inner_cols(rhs), [j for j in range(leaves) if edge <= j < leaves - edge]),
    )

    gathered = [gather(x) for x, _ in chunks]

    def swapped(block):
        sent = block(send_order)
        return partner(sent)

    def kept(block):
        return block(keep_order)

    places = (ancestor_rows - me * anc).astype(jnp.int32)
    cpl_block = lambda order: select_rows(couple, places, order, rows)
    a_swap = swapped(lambda order: pick(inverse, order, rows))
    a_keep = kept(lambda order: pick(inverse, order, rows))
    c_swap = swapped(cpl_block)
    c_keep = kept(cpl_block)

    solved = []
    for pieces in gathered:
        own, other = partials(a_keep, a_swap, pieces)
        other = partner(other)
        solved.append((own + other.astype(F32)).astype(BF16))

    shares = []
    for (_, dests), y in zip(chunks, solved):
        pieces = gather(y)
        own, other = partials(c_keep, c_swap, pieces)
        q = own + partner(other).astype(F32)

        def piece(target):
            place = sum(jnp.where(target == j, i, 0) for i, j in enumerate(dests))
            return lax.dynamic_slice_in_dim(q, place * narrow, narrow, 1)

        total = piece(leaf)
        for d in range(1, leaves):
            sent = piece(leaf ^ d).astype(BF16)
            got = lax.ppermute(sent, "leaf", [(j ^ d, j) for j in dests])
            total = total + got.astype(F32)
        shares.append(total)

    out = ancestor_rhs - jnp.where(inner, shares[1], shares[0])
    y_outer, y_inner = solved
    solution = jnp.concatenate([y_outer[:, :cut], y_inner, y_outer[:, cut:]], axis=1)
    return (solution[None], out)


def solution(mesh):
    return jax.shard_map(
        on_device,
        mesh=mesh,
        in_specs=(
            P("leaf", "row", None),
            P("leaf", "row", None),
            P("leaf", "row", None),
            P("leaf", "row"),
            P("row", "leaf"),
        ),
        out_specs=(P("leaf", "row", None), P("row", "leaf")),
        check_vma=False,
    )
```

```python
import functools

import jax
import jax.numpy as jnp
import numpy as np
from jax import lax
from jax.experimental import pallas as pl
from jax.experimental.pallas import tpu as pltpu
from jax.sharding import PartitionSpec as P

VMEM = pl.BlockSpec(memory_space=pltpu.VMEM)
SMEM = pl.BlockSpec(memory_space=pltpu.SMEM)
SPLIT = 4
F32 = jnp.float32
BF16 = jnp.bfloat16


def block_copies(first, n, index, src, out, sem):
    width = out.shape[1] // n
    rows = out.shape[0] // SPLIT
    copies = []
    for j in range(n):
        start = pl.multiple_of(index[0, first + j] * width, 128)
        copies.append(
            [
                pltpu.make_async_copy(
                    src.at[pl.ds(r * rows, rows), pl.ds(start, width)],
                    out.at[pl.ds(r * rows, rows), pl.ds(j * width, width)],
                    sem.at[j, r],
                )
                for r in range(SPLIT)
            ]
        )
    return copies


def pick_kernel(first, n, index, src, out, sem):
    copies = block_copies(first, n, index, src, out, sem)
    for group in copies:
        for copy in group:
            copy.start()
    for group in copies:
        for copy in group:
            copy.wait()


def column_block(src, start, width):
    return lax.dynamic_slice_in_dim(src, start * width, width, 1)


def pick(index, first, n, src, width):
    if width % 128:
        blocks = [column_block(src, index[0, first + j], width) for j in range(n)]
        return jnp.concatenate(blocks, axis=1)
    return pl.pallas_call(
        functools.partial(pick_kernel, first, n),
        out_shape=jax.ShapeDtypeStruct((src.shape[0], n * width), src.dtype),
        in_specs=[SMEM, pl.BlockSpec(memory_space=pltpu.HBM)],
        out_specs=VMEM,
        scratch_shapes=[pltpu.SemaphoreType.DMA((n, SPLIT))],
        compiler_params=pltpu.CompilerParams(vmem_limit_bytes=8 << 20),
        name="pick",
    )(index, pltpu.with_memory_space_constraint(src, pltpu.HBM))


def select_kernel(first, n, base, index, places, src, out, buf, sem):
    rows, width = buf.shape[0], buf.shape[1] // n
    copies = block_copies(first, n, index, src, buf, sem)
    for group in copies:
        for copy in group:
            copy.start()
    hot = lax.broadcasted_iota(jnp.int32, (rows, rows), 0) + index[0, base] == places[...]
    hot = jnp.where(hot, 1.0, 0.0).astype(BF16)
    for j, group in enumerate(copies):
        for copy in group:
            copy.wait()
        block = slice(j * width, (j + 1) * width)
        out[:, block] = jnp.dot(hot, buf[:, block], preferred_element_type=F32).astype(BF16)


def select_rows(index, first, n, base, src, places, width):
    rows = src.shape[0]
    if width % 128:
        hot = lax.broadcasted_iota(jnp.int32, (rows, rows), 0) + index[0, base] == places
        return hot.astype(src.dtype) @ pick(index, first, n, src, width)
    return pl.pallas_call(
        functools.partial(select_kernel, first, n, base),
        out_shape=jax.ShapeDtypeStruct((rows, n * width), src.dtype),
        in_specs=[SMEM, VMEM, pl.BlockSpec(memory_space=pltpu.HBM)],
        out_specs=VMEM,
        scratch_shapes=[
            pltpu.VMEM((rows, n * width), src.dtype),
            pltpu.SemaphoreType.DMA((n, SPLIT)),
        ],
        compiler_params=pltpu.CompilerParams(vmem_limit_bytes=12 << 20),
        name="select_rows",
    )(index, places, pltpu.with_memory_space_constraint(src, pltpu.HBM))


def partial_kernel(n, keep, swap, *refs):
    pieces, (own, other, joined) = refs[:n], refs[n:]
    depth = pieces[0].shape[0]
    for j in range(n):
        joined[j * depth : (j + 1) * depth, :] = pieces[j][...]
    other[...] = jnp.dot(swap[...], joined[...], preferred_element_type=F32).astype(BF16)
    own[...] = jnp.dot(keep[...], joined[...], preferred_element_type=F32)


def partials(keep, swap, pieces):
    n = len(pieces)
    rows, depth = keep.shape
    width = pieces[0].shape[1]
    return pl.pallas_call(
        functools.partial(partial_kernel, n),
        out_shape=(
            jax.ShapeDtypeStruct((rows, width), F32),
            jax.ShapeDtypeStruct((rows, width), BF16),
        ),
        in_specs=[VMEM] * (2 + n),
        out_specs=(VMEM, VMEM),
        scratch_shapes=[pltpu.VMEM((depth, width), BF16)],
        compiler_params=pltpu.CompilerParams(vmem_limit_bytes=12 << 20),
        name="partials",
    )(keep, swap, *pieces)


def split_kernel(first, narrow, index, own, other, total, *pieces):
    for d in range(len(pieces) + 1):
        start = pl.multiple_of(index[0, first + d] * narrow, 128)
        piece = own[:, pl.ds(start, narrow)] + other[:, pl.ds(start, narrow)].astype(F32)
        if d == 0:
            total[...] = piece
        else:
            pieces[d - 1][...] = piece.astype(BF16)


def split(index, first, leaves, narrow, own, other):
    rows = own.shape[0]
    if narrow % 128:
        q = own + other.astype(F32)
        blocks = [column_block(q, index[0, first + d], narrow) for d in range(leaves)]
        return blocks[0], *[block.astype(BF16) for block in blocks[1:]]
    return pl.pallas_call(
        functools.partial(split_kernel, first, narrow),
        out_shape=[jax.ShapeDtypeStruct((rows, narrow), F32)]
        + [jax.ShapeDtypeStruct((rows, narrow), BF16)] * (leaves - 1),
        in_specs=[SMEM, VMEM, VMEM],
        out_specs=[VMEM] * leaves,
        compiler_params=pltpu.CompilerParams(vmem_limit_bytes=6 << 20),
        name="split",
    )(index, own, other)


def finish_kernel(which, index, rhs, *refs):
    groups, out = refs[:-1], refs[-1]
    n = len(groups) // 2
    for c in (0, 1):

        @pl.when(index[0, which] == c)
        def _():
            group = groups[c * n : (c + 1) * n]
            out[...] = rhs[...] - sum((g[...].astype(F32) for g in group[1:]), group[0][...])


def finish(index, which, rhs, groups):
    return pl.pallas_call(
        functools.partial(finish_kernel, which),
        out_shape=jax.ShapeDtypeStruct(rhs.shape, F32),
        in_specs=[SMEM] + [VMEM] * (1 + sum(len(g) for g in groups)),
        out_specs=VMEM,
        compiler_params=pltpu.CompilerParams(vmem_limit_bytes=8 << 20),
        name="finish",
    )(index, rhs, *[x for g in groups for x in g])


def on_device(sep_inverse, rhs_block, coupling, ancestor_rows, ancestor_rhs):
    inverse, rhs, couple = sep_inverse[0], rhs_block[0], coupling[0]
    leaves, n_row = lax.axis_size("leaf"), lax.axis_size("row")
    rows = inverse.shape[0]
    anc = couple.shape[0]
    width = rhs.shape[1]
    narrow = width // leaves
    dims = [1 << b for b in range(1, n_row.bit_length() - 1)]
    routes = (dims, dims[::-1])
    masks = ([0], [0])
    for step in range(len(dims)):
        for k in (0, 1):
            masks[k].extend([m ^ routes[k][step] for m in masks[k]])
    n = len(masks[0])
    edge = leaves // 4
    cut = edge * narrow
    is_inner = lambda j: edge <= j < leaves - edge
    dests = [[j for j in range(leaves) if is_inner(j) == bool(c)] for c in (0, 1)]

    table = []
    for leaf in range(leaves):
        for me in range(n_row):
            line = [(me ^ 1) ^ m for m in masks[1 - (me & 1)]]
            line += [me ^ m for m in masks[me & 1]]
            line.append(me * anc)
            for group in dests:
                line += [group.index(leaf ^ d) if leaf ^ d in group else 0 for d in range(leaves)]
            line.append(int(is_inner(leaf)))
            table.append(line)
    table = jnp.array(np.array(table, np.int32))
    device = lax.axis_index(("leaf", "row"))
    index = lax.dynamic_slice(table, (device, jnp.zeros_like(device)), (1, table.shape[1]))
    index, rhs = lax.optimization_barrier((index, rhs))
    base = 2 * n
    first_place = lambda c: base + 1 + c * leaves
    which = base + 1 + 2 * leaves

    def partner(x):
        return lax.ppermute(x, "row", [(i, i ^ 1) for i in range(n_row)])

    def gather(x):
        pieces = [x]
        for step in range(len(dims)):
            pairs = [(i, i ^ routes[i & 1][step]) for i in range(n_row)]
            for p in range(len(pieces)):
                pieces.append(lax.ppermute(pieces[p], "row", pairs))
        return pieces

    chunks = (
        jnp.concatenate([rhs[:, :cut], rhs[:, width - cut :]], axis=1),
        rhs[:, cut : width - cut],
    )
    gathered = [gather(x) for x in chunks]

    def inv_block(first):
        return pick(index, first, n, inverse, rows)

    def cpl_block(first):
        return select_rows(index, first, n, base, couple, ancestor_rows, rows)

    def both(block):
        sent = block(0)
        kept = block(n)
        return kept, partner(sent)

    inv = both(inv_block)
    cpl = both(cpl_block)

    solved = []
    for pieces in gathered:
        own, other = partials(*inv, pieces)
        other = partner(other)
        solved.append((own + other.astype(F32)).astype(BF16))

    shares = []
    for c, y in enumerate(solved):
        pieces = gather(y)
        own, other = partials(*cpl, pieces)
        other = partner(other)
        total, *sent = split(index, first_place(c), leaves, narrow, own, other)
        group = [total]
        for d in range(1, leaves):
            group.append(lax.ppermute(sent[d - 1], "leaf", [(j ^ d, j) for j in dests[c]]))
        shares.append(group)

    y_outer, y_inner = solved
    solution = jnp.concatenate([y_outer[:, :cut], y_inner, y_outer[:, cut:]], axis=1)
    out = finish(index, which, ancestor_rhs, shares)
    return (solution[None], out)


def solution(mesh):
    return jax.shard_map(
        on_device,
        mesh=mesh,
        in_specs=(
            P("leaf", "row", None),
            P("leaf", "row", None),
            P("leaf", "row", None),
            P("leaf", "row"),
            P("row", "leaf"),
        ),
        out_specs=(P("leaf", "row", None), P("row", "leaf")),
        check_vma=False,
    )
```

```python
import functools

import jax
import jax.numpy as jnp
import numpy as np
from jax import lax
from jax.experimental import pallas as pl
from jax.experimental.pallas import tpu as pltpu
from jax.sharding import PartitionSpec as P

VMEM = pl.BlockSpec(memory_space=pltpu.VMEM)
SMEM = pl.BlockSpec(memory_space=pltpu.SMEM)
SPLIT = 4
F32 = jnp.float32
BF16 = jnp.bfloat16


def block_copies(first, n, index, src, out, sem):
    width = out.shape[1] // n
    rows = out.shape[0] // SPLIT
    copies = []
    for j in range(n):
        start = pl.multiple_of(index[0, first + j] * width, 128)
        copies.append(
            [
                pltpu.make_async_copy(
                    src.at[pl.ds(r * rows, rows), pl.ds(start, width)],
                    out.at[pl.ds(r * rows, rows), pl.ds(j * width, width)],
                    sem.at[j, r],
                )
                for r in range(SPLIT)
            ]
        )
    return copies


def pick_kernel(first, n, index, src, out, sem):
    copies = block_copies(first, n, index, src, out, sem)
    for group in copies:
        for copy in group:
            copy.start()
    for group in copies:
        for copy in group:
            copy.wait()


def column_block(src, start, width):
    return lax.dynamic_slice_in_dim(src, start * width, width, 1)


def pick(index, first, n, src, width, space=None):
    if width % 128:
        blocks = [column_block(src, index[0, first + j], width) for j in range(n)]
        return jnp.concatenate(blocks, axis=1)
    if space is not None:
        src = pltpu.with_memory_space_constraint(src, space)
    return pl.pallas_call(
        functools.partial(pick_kernel, first, n),
        out_shape=jax.ShapeDtypeStruct((src.shape[0], n * width), src.dtype),
        in_specs=[SMEM, pl.BlockSpec(memory_space=pl.ANY)],
        out_specs=VMEM,
        scratch_shapes=[pltpu.SemaphoreType.DMA((n, SPLIT))],
        compiler_params=pltpu.CompilerParams(vmem_limit_bytes=8 << 20),
        name="pick",
    )(index, src)


def select_kernel(first, n, base, index, places, src, out, buf, sem):
    rows, width = buf.shape[0], buf.shape[1] // n
    copies = block_copies(first, n, index, src, buf, sem)
    for group in copies:
        for copy in group:
            copy.start()
    hot = lax.broadcasted_iota(jnp.int32, (rows, rows), 0) + index[0, base] == places[...]
    hot = jnp.where(hot, 1.0, 0.0).astype(BF16)
    for j, group in enumerate(copies):
        for copy in group:
            copy.wait()
        block = slice(j * width, (j + 1) * width)
        out[:, block] = jnp.dot(hot, buf[:, block], preferred_element_type=F32).astype(BF16)


def select_rows(index, first, n, base, src, places, width):
    rows = src.shape[0]
    if width % 128:
        hot = lax.broadcasted_iota(jnp.int32, (rows, rows), 0) + index[0, base] == places
        return hot.astype(src.dtype) @ pick(index, first, n, src, width)
    return pl.pallas_call(
        functools.partial(select_kernel, first, n, base),
        out_shape=jax.ShapeDtypeStruct((rows, n * width), src.dtype),
        in_specs=[SMEM, VMEM, pl.BlockSpec(memory_space=pl.ANY)],
        out_specs=VMEM,
        scratch_shapes=[
            pltpu.VMEM((rows, n * width), src.dtype),
            pltpu.SemaphoreType.DMA((n, SPLIT)),
        ],
        compiler_params=pltpu.CompilerParams(vmem_limit_bytes=12 << 20),
        name="select_rows",
    )(index, places, src)


def partial_kernel(n, keep, swap, *refs):
    pieces, (own, other, joined) = refs[:n], refs[n:]
    depth = pieces[0].shape[0]
    for j in range(n):
        joined[j * depth : (j + 1) * depth, :] = pieces[j][...]
    other[...] = jnp.dot(swap[...], joined[...], preferred_element_type=F32).astype(BF16)
    own[...] = jnp.dot(keep[...], joined[...], preferred_element_type=F32)


def partials(keep, swap, pieces):
    n = len(pieces)
    rows, depth = keep.shape
    width = pieces[0].shape[1]
    return pl.pallas_call(
        functools.partial(partial_kernel, n),
        out_shape=(
            jax.ShapeDtypeStruct((rows, width), F32),
            jax.ShapeDtypeStruct((rows, width), BF16),
        ),
        in_specs=[VMEM] * (2 + n),
        out_specs=(VMEM, VMEM),
        scratch_shapes=[pltpu.VMEM((depth, width), BF16)],
        compiler_params=pltpu.CompilerParams(vmem_limit_bytes=12 << 20),
        name="partials",
    )(keep, swap, *pieces)


def split_kernel(first, narrow, index, own, other, total, *pieces):
    for d in range(len(pieces) + 1):
        start = pl.multiple_of(index[0, first + d] * narrow, 128)
        piece = own[:, pl.ds(start, narrow)] + other[:, pl.ds(start, narrow)].astype(F32)
        if d == 0:
            total[...] = piece
        else:
            pieces[d - 1][...] = piece.astype(BF16)


def split(index, first, leaves, narrow, own, other):
    rows = own.shape[0]
    if narrow % 128:
        q = own + other.astype(F32)
        blocks = [column_block(q, index[0, first + d], narrow) for d in range(leaves)]
        return blocks[0], *[block.astype(BF16) for block in blocks[1:]]
    return pl.pallas_call(
        functools.partial(split_kernel, first, narrow),
        out_shape=[jax.ShapeDtypeStruct((rows, narrow), F32)]
        + [jax.ShapeDtypeStruct((rows, narrow), BF16)] * (leaves - 1),
        in_specs=[SMEM, VMEM, VMEM],
        out_specs=[VMEM] * leaves,
        compiler_params=pltpu.CompilerParams(vmem_limit_bytes=6 << 20),
        name="split",
    )(index, own, other)


def finish_kernel(which, index, rhs, *refs):
    groups, out = refs[:-1], refs[-1]
    n = len(groups) // 2
    for c in (0, 1):

        @pl.when(index[0, which] == c)
        def _():
            group = groups[c * n : (c + 1) * n]
            out[...] = rhs[...] - sum((g[...].astype(F32) for g in group[1:]), group[0][...])


def finish(index, which, rhs, groups):
    return pl.pallas_call(
        functools.partial(finish_kernel, which),
        out_shape=jax.ShapeDtypeStruct(rhs.shape, F32),
        in_specs=[SMEM] + [VMEM] * (1 + sum(len(g) for g in groups)),
        out_specs=VMEM,
        compiler_params=pltpu.CompilerParams(vmem_limit_bytes=8 << 20),
        name="finish",
    )(index, rhs, *[x for g in groups for x in g])


def on_device(sep_inverse, rhs_block, coupling, ancestor_rows, ancestor_rhs):
    inverse, rhs, couple = sep_inverse[0], rhs_block[0], coupling[0]
    leaves, n_row = lax.axis_size("leaf"), lax.axis_size("row")
    rows = inverse.shape[0]
    anc = couple.shape[0]
    width = rhs.shape[1]
    narrow = width // leaves
    dims = [1 << b for b in range(1, n_row.bit_length() - 1)]
    routes = (dims, dims[::-1])
    masks = ([0], [0])
    for step in range(len(dims)):
        for k in (0, 1):
            masks[k].extend([m ^ routes[k][step] for m in masks[k]])
    n = len(masks[0])
    edge = leaves // 4
    cut = edge * narrow
    is_inner = lambda j: edge <= j < leaves - edge
    dests = [[j for j in range(leaves) if is_inner(j) == bool(c)] for c in (0, 1)]

    table = []
    for leaf in range(leaves):
        for me in range(n_row):
            line = [(me ^ 1) ^ m for m in masks[1 - (me & 1)]]
            line += [me ^ m for m in masks[me & 1]]
            line.append(me * anc)
            for group in dests:
                line += [group.index(leaf ^ d) if leaf ^ d in group else 0 for d in range(leaves)]
            line.append(int(is_inner(leaf)))
            table.append(line)
    table = jnp.array(np.array(table, np.int32))
    device = lax.axis_index(("leaf", "row"))
    index = lax.dynamic_slice(table, (device, jnp.zeros_like(device)), (1, table.shape[1]))
    index, rhs = lax.optimization_barrier((index, rhs))
    base = 2 * n
    first_place = lambda c: base + 1 + c * leaves
    which = base + 1 + 2 * leaves

    def partner(x):
        return lax.ppermute(x, "row", [(i, i ^ 1) for i in range(n_row)])

    def gather(x):
        pieces = [x]
        for step in range(len(dims)):
            pairs = [(i, i ^ routes[i & 1][step]) for i in range(n_row)]
            for p in range(len(pieces)):
                pieces.append(lax.ppermute(pieces[p], "row", pairs))
        return pieces

    chunks = (
        jnp.concatenate([rhs[:, :cut], rhs[:, width - cut :]], axis=1),
        rhs[:, cut : width - cut],
    )
    gathered = [gather(x) for x in chunks]

    def inv_block(first, space):
        return pick(index, first, n, inverse, rows, space)

    def cpl_block(first, space):
        return select_rows(index, first, n, base, couple, ancestor_rows, rows)

    def both(block):
        sent = block(0, pltpu.HBM)
        kept = block(n, None)
        return kept, partner(sent)

    inv = both(inv_block)
    cpl = both(cpl_block)

    solved = []
    for pieces in gathered:
        own, other = partials(*inv, pieces)
        other = partner(other)
        solved.append((own + other.astype(F32)).astype(BF16))

    shares = []
    for c, y in enumerate(solved):
        pieces = gather(y)
        own, other = partials(*cpl, pieces)
        other = partner(other)
        total, *sent = split(index, first_place(c), leaves, narrow, own, other)
        group = [total]
        for d in range(1, leaves):
            group.append(lax.ppermute(sent[d - 1], "leaf", [(j ^ d, j) for j in dests[c]]))
        shares.append(group)

    y_outer, y_inner = solved
    solution = jnp.concatenate([y_outer[:, :cut], y_inner, y_outer[:, cut:]], axis=1)
    out = finish(index, which, ancestor_rhs, shares)
    return (solution[None], out)


def solution(mesh):
    return jax.shard_map(
        on_device,
        mesh=mesh,
        in_specs=(
            P("leaf", "row", None),
            P("leaf", "row", None),
            P("leaf", "row", None),
            P("leaf", "row"),
            P("row", "leaf"),
        ),
        out_specs=(P("leaf", "row", None), P("row", "leaf")),
        check_vma=False,
    )
```

```python
import functools

import jax
import jax.numpy as jnp
from jax import lax
from jax.experimental import pallas as pl
from jax.experimental.pallas import tpu as pltpu
from jax.sharding import PartitionSpec as P

VMEM = pl.BlockSpec(memory_space=pltpu.VMEM)
SPLIT = 4
F32 = jnp.float32
BF16 = jnp.bfloat16


def block_of(masks, other, j):
    me = lax.axis_index("row")
    core = me & 1
    if other:
        me, core = me ^ 1, 1 - core
    return me ^ jnp.where(core == 0, masks[0][j], masks[1][j])


def block_copies(masks, other, src, out, sem):
    n = len(masks[0])
    width = out.shape[1] // n
    rows = out.shape[0] // SPLIT
    copies = []
    for j in range(n):
        start = pl.multiple_of(block_of(masks, other, j) * width, 128)
        copies.append(
            [
                pltpu.make_async_copy(
                    src.at[pl.ds(r * rows, rows), pl.ds(start, width)],
                    out.at[pl.ds(r * rows, rows), pl.ds(j * width, width)],
                    sem.at[j, r],
                )
                for r in range(SPLIT)
            ]
        )
    return copies


def pick_kernel(masks, other, src, out, sem):
    copies = block_copies(masks, other, src, out, sem)
    for group in copies:
        for copy in group:
            copy.start()
    for group in copies:
        for copy in group:
            copy.wait()


def column_block(src, start, width):
    return lax.dynamic_slice_in_dim(src, start * width, width, 1)


def pick(masks, other, src, width):
    n = len(masks[0])
    if width % 128:
        blocks = [column_block(src, block_of(masks, other, j), width) for j in range(n)]
        return jnp.concatenate(blocks, axis=1)
    if other:
        src = pltpu.with_memory_space_constraint(src, pltpu.HBM)
    return pl.pallas_call(
        functools.partial(pick_kernel, masks, other),
        out_shape=jax.ShapeDtypeStruct((src.shape[0], n * width), src.dtype),
        in_specs=[pl.BlockSpec(memory_space=pl.ANY)],
        out_specs=VMEM,
        scratch_shapes=[pltpu.SemaphoreType.DMA((n, SPLIT))],
        compiler_params=pltpu.CompilerParams(vmem_limit_bytes=8 << 20),
        name="pick",
    )(src)


def one_hot(places, rows):
    first = lax.axis_index("row") * rows
    return lax.broadcasted_iota(jnp.int32, (rows, rows), 0) + first == places


def select_kernel(masks, other, places, src, out, buf, sem):
    rows, n = buf.shape[0], len(masks[0])
    width = buf.shape[1] // n
    copies = block_copies(masks, other, src, buf, sem)
    for group in copies:
        for copy in group:
            copy.start()
    hot = jnp.where(one_hot(places[...], rows), 1.0, 0.0).astype(BF16)
    for j, group in enumerate(copies):
        for copy in group:
            copy.wait()
        block = slice(j * width, (j + 1) * width)
        out[:, block] = jnp.dot(hot, buf[:, block], preferred_element_type=F32).astype(BF16)


def select_rows(masks, other, src, places, width):
    rows, n = src.shape[0], len(masks[0])
    if width % 128:
        return one_hot(places, rows).astype(src.dtype) @ pick(masks, other, src, width)
    return pl.pallas_call(
        functools.partial(select_kernel, masks, other),
        out_shape=jax.ShapeDtypeStruct((rows, n * width), src.dtype),
        in_specs=[VMEM, pl.BlockSpec(memory_space=pl.ANY)],
        out_specs=VMEM,
        scratch_shapes=[
            pltpu.VMEM((rows, n * width), src.dtype),
            pltpu.SemaphoreType.DMA((n, SPLIT)),
        ],
        compiler_params=pltpu.CompilerParams(vmem_limit_bytes=12 << 20),
        name="select_rows",
    )(places, src)


def partial_kernel(n, first, had, keep, swap, *refs):
    pieces, sums, (own, other, joined) = refs[:n], refs[n : n + 2 * had], refs[n + 2 * had :]
    depth = pieces[0].shape[0]
    for j in range(n):
        joined[j * depth : (j + 1) * depth, :] = pieces[j][...]
    columns = slice(first * depth, (first + n) * depth)
    for k, (block, out) in enumerate(((keep, own), (swap, other))):
        value = jnp.dot(block[:, columns], joined[...], preferred_element_type=F32)
        if had:
            value = value + sums[k][...]
        out[...] = value.astype(out.dtype)


def partials(keep, swap, pieces, first=0, sums=(), other_type=BF16):
    n = len(pieces)
    rows = keep.shape[0]
    depth, width = pieces[0].shape
    return pl.pallas_call(
        functools.partial(partial_kernel, n, first, bool(sums)),
        out_shape=(
            jax.ShapeDtypeStruct((rows, width), F32),
            jax.ShapeDtypeStruct((rows, width), other_type),
        ),
        in_specs=[VMEM] * (2 + n + len(sums)),
        out_specs=(VMEM, VMEM),
        scratch_shapes=[pltpu.VMEM((n * depth, width), BF16)],
        compiler_params=pltpu.CompilerParams(vmem_limit_bytes=12 << 20),
        name="partials",
    )(keep, swap, *pieces, *sums)


def place_of(group, leaf):
    return sum(jnp.where(leaf == j, i, 0) for i, j in enumerate(group))


def member(group, leaf):
    return sum(jnp.where(leaf == j, 1.0, 0.0) for j in group)


def split_kernel(group, narrow, own, other, total, *pieces):
    leaf = lax.axis_index("leaf")
    for d in range(len(pieces) + 1):
        start = pl.multiple_of(place_of(group, leaf ^ d) * narrow, 128)
        piece = own[:, pl.ds(start, narrow)] + other[:, pl.ds(start, narrow)].astype(F32)
        if d == 0:
            total[...] = jnp.where(member(group, leaf) > 0, piece, 0.0)
        else:
            pieces[d - 1][...] = piece.astype(BF16)


def split(group, leaves, narrow, own, other):
    rows = own.shape[0]
    if narrow % 128:
        leaf = lax.axis_index("leaf")
        q = own + other.astype(F32)
        blocks = [column_block(q, place_of(group, leaf ^ d), narrow) for d in range(leaves)]
        total = jnp.where(member(group, leaf) > 0, blocks[0], 0.0)
        return total, *[block.astype(BF16) for block in blocks[1:]]
    return pl.pallas_call(
        functools.partial(split_kernel, group, narrow),
        out_shape=[jax.ShapeDtypeStruct((rows, narrow), F32)]
        + [jax.ShapeDtypeStruct((rows, narrow), BF16)] * (leaves - 1),
        in_specs=[VMEM, VMEM],
        out_specs=[VMEM] * leaves,
        compiler_params=pltpu.CompilerParams(vmem_limit_bytes=6 << 20),
        name="split",
    )(own, other)


def on_device(sep_inverse, rhs_block, coupling, ancestor_rows, ancestor_rhs):
    inverse, rhs, couple = sep_inverse[0], rhs_block[0], coupling[0]
    leaves, n_row = lax.axis_size("leaf"), lax.axis_size("row")
    rows = inverse.shape[0]
    width = rhs.shape[1]
    narrow = width // leaves
    dims = [1 << b for b in range(1, n_row.bit_length() - 1)]
    routes = (dims, dims[::-1])
    masks = ([0], [0])
    for step in range(len(dims)):
        for k in (0, 1):
            masks[k].extend([m ^ routes[k][step] for m in masks[k]])
    edge = leaves // 4
    cut = edge * narrow
    is_inner = lambda j: edge <= j < leaves - edge
    dests = [[j for j in range(leaves) if is_inner(j) == bool(c)] for c in (0, 1)]

    def partner(x):
        return lax.ppermute(x, "row", [(i, i ^ 1) for i in range(n_row)])

    def gather(x):
        pieces = [x]
        for step in range(len(dims)):
            pairs = [(i, i ^ routes[i & 1][step]) for i in range(n_row)]
            for p in range(len(pieces)):
                pieces.append(lax.ppermute(pieces[p], "row", pairs))
        return pieces

    chunks = (
        jnp.concatenate([rhs[:, :cut], rhs[:, width - cut :]], axis=1),
        rhs[:, cut : width - cut],
    )
    gathered = [gather(x) for x in chunks]

    def inv_block(other):
        return pick(masks, other, inverse, rows)

    def cpl_block(other):
        return select_rows(masks, other, couple, ancestor_rows, rows)

    def both(block):
        sent = block(True)
        kept = block(False)
        return kept, partner(sent)

    inv = both(inv_block)
    cpl = both(cpl_block)

    solved = []
    for pieces in gathered:
        own, other = partials(*inv, pieces)
        other = partner(other)
        solved.append((own + other.astype(F32)).astype(BF16))

    out = ancestor_rhs
    for c, y in enumerate(solved):
        pieces = gather(y)
        sums = ()
        if c:
            sums = partials(*cpl, pieces[:-1], other_type=F32)
        first = len(pieces) - 1 if c else 0
        own, other = partials(*cpl, pieces[first:], first, sums)
        other = partner(other)
        total, *sent = split(dests[c], leaves, narrow, own, other)
        for d in range(1, leaves):
            got = lax.ppermute(sent[d - 1], "leaf", [(j ^ d, j) for j in dests[c]])
            total = total + got.astype(F32)
        out = out - total

    y_outer, y_inner = solved
    solution = jnp.concatenate([y_outer[:, :cut], y_inner, y_outer[:, cut:]], axis=1)
    return (solution[None], out)


def solution(mesh):
    return jax.shard_map(
        on_device,
        mesh=mesh,
        in_specs=(
            P("leaf", "row", None),
            P("leaf", "row", None),
            P("leaf", "row", None),
            P("leaf", "row"),
            P("row", "leaf"),
        ),
        out_specs=(P("leaf", "row", None), P("row", "leaf")),
        check_vma=False,
    )
```

```python
import functools

import jax
import jax.numpy as jnp
from jax import lax
from jax.experimental import pallas as pl
from jax.experimental.pallas import tpu as pltpu
from jax.sharding import PartitionSpec as P

VMEM = pl.BlockSpec(memory_space=pltpu.VMEM)
SPLIT = 4
F32 = jnp.float32
BF16 = jnp.bfloat16


def block_of(masks, other, j):
    me = lax.axis_index("row")
    core = me & 1
    if other:
        me, core = me ^ 1, 1 - core
    return me ^ jnp.where(core == 0, masks[0][j], masks[1][j])


def block_copies(masks, other, src, out, sem):
    n = len(masks[0])
    width = out.shape[1] // n
    rows = out.shape[0] // SPLIT
    copies = []
    for j in range(n):
        start = pl.multiple_of(block_of(masks, other, j) * width, 128)
        copies.append(
            [
                pltpu.make_async_copy(
                    src.at[pl.ds(r * rows, rows), pl.ds(start, width)],
                    out.at[pl.ds(r * rows, rows), pl.ds(j * width, width)],
                    sem.at[j, r],
                )
                for r in range(SPLIT)
            ]
        )
    return copies


def pick_kernel(masks, other, src, out, sem):
    copies = block_copies(masks, other, src, out, sem)
    for group in copies:
        for copy in group:
            copy.start()
    for group in copies:
        for copy in group:
            copy.wait()


def column_block(src, start, width):
    return lax.dynamic_slice_in_dim(src, start * width, width, 1)


def pick(masks, other, src, width):
    n = len(masks[0])
    if width % 128:
        blocks = [column_block(src, block_of(masks, other, j), width) for j in range(n)]
        return jnp.concatenate(blocks, axis=1)
    if other:
        src = pltpu.with_memory_space_constraint(src, pltpu.HBM)
    return pl.pallas_call(
        functools.partial(pick_kernel, masks, other),
        out_shape=jax.ShapeDtypeStruct((src.shape[0], n * width), src.dtype),
        in_specs=[pl.BlockSpec(memory_space=pl.ANY)],
        out_specs=VMEM,
        scratch_shapes=[pltpu.SemaphoreType.DMA((n, SPLIT))],
        compiler_params=pltpu.CompilerParams(vmem_limit_bytes=8 << 20),
        name="pick",
    )(src)


def one_hot(places, rows):
    first = lax.axis_index("row") * rows
    return lax.broadcasted_iota(jnp.int32, (rows, rows), 0) + first == places


def select_kernel(masks, other, places, src, out, buf, sem):
    rows, n = buf.shape[0], len(masks[0])
    width = buf.shape[1] // n
    copies = block_copies(masks, other, src, buf, sem)
    for group in copies:
        for copy in group:
            copy.start()
    hot = jnp.where(one_hot(places[...], rows), 1.0, 0.0).astype(BF16)
    for j, group in enumerate(copies):
        for copy in group:
            copy.wait()
        block = slice(j * width, (j + 1) * width)
        out[:, block] = jnp.dot(hot, buf[:, block], preferred_element_type=F32).astype(BF16)


def select_rows(masks, other, src, places, width):
    rows, n = src.shape[0], len(masks[0])
    if width % 128:
        return one_hot(places, rows).astype(src.dtype) @ pick(masks, other, src, width)
    return pl.pallas_call(
        functools.partial(select_kernel, masks, other),
        out_shape=jax.ShapeDtypeStruct((rows, n * width), src.dtype),
        in_specs=[VMEM, pl.BlockSpec(memory_space=pl.ANY)],
        out_specs=VMEM,
        scratch_shapes=[
            pltpu.VMEM((rows, n * width), src.dtype),
            pltpu.SemaphoreType.DMA((n, SPLIT)),
        ],
        compiler_params=pltpu.CompilerParams(vmem_limit_bytes=12 << 20),
        name="select_rows",
    )(places, src)


def partial_kernel(n, first, had, keep, swap, *refs):
    pieces, sums, (own, other, joined) = refs[:n], refs[n : n + 2 * had], refs[n + 2 * had :]
    depth = pieces[0].shape[0]
    for j in range(n):
        joined[j * depth : (j + 1) * depth, :] = pieces[j][...]
    columns = slice(first * depth, (first + n) * depth)
    for k, (block, out) in enumerate(((keep, own), (swap, other))):
        value = jnp.dot(block[:, columns], joined[...], preferred_element_type=F32)
        if had:
            value = value + sums[k][...]
        out[...] = value.astype(out.dtype)


def partials(keep, swap, pieces, first=0, sums=(), other_type=BF16):
    n = len(pieces)
    rows = keep.shape[0]
    depth, width = pieces[0].shape
    return pl.pallas_call(
        functools.partial(partial_kernel, n, first, bool(sums)),
        out_shape=(
            jax.ShapeDtypeStruct((rows, width), F32),
            jax.ShapeDtypeStruct((rows, width), other_type),
        ),
        in_specs=[VMEM] * (2 + n + len(sums)),
        out_specs=(VMEM, VMEM),
        scratch_shapes=[pltpu.VMEM((n * depth, width), BF16)],
        compiler_params=pltpu.CompilerParams(vmem_limit_bytes=12 << 20),
        name="partials",
    )(keep, swap, *pieces, *sums)


def swap_halves(x):
    return pltpu.roll(x, x.shape[1] // 2, 1)


def low_lanes(shape):
    return lax.broadcasted_iota(jnp.int32, shape, 1) < shape[1] // 2


def tile(t):
    return slice(t * 128, (t + 1) * 128)


def chunk_kernel(c, x, out):
    for t in range(out.shape[1] // 128):
        a, b = x[:, tile(2 * t)].astype(F32), x[:, tile(2 * t + 1)].astype(F32)
        low = low_lanes(a.shape)
        both = jnp.where(low, swap_halves(a), b) if c else jnp.where(low, a, swap_halves(b))
        out[:, tile(t)] = both.astype(out.dtype)


def chunk(x, c, leaves):
    rows, width = x.shape
    half = width // leaves // 2
    if half != 64:
        return x.reshape(rows, leaves, 2, half)[:, :, c].reshape(rows, width // 2)
    return pl.pallas_call(
        functools.partial(chunk_kernel, c),
        out_shape=jax.ShapeDtypeStruct((rows, width // 2), x.dtype),
        in_specs=[VMEM],
        out_specs=VMEM,
        compiler_params=pltpu.CompilerParams(vmem_limit_bytes=4 << 20),
        name="chunk",
    )(x)


def join_kernel(x, y, out):
    for t in range(x.shape[1] // 128):
        a, b = x[:, tile(t)].astype(F32), y[:, tile(t)].astype(F32)
        low = low_lanes(a.shape)
        out[:, tile(2 * t)] = jnp.where(low, a, swap_halves(b)).astype(out.dtype)
        out[:, tile(2 * t + 1)] = jnp.where(low, swap_halves(a), b).astype(out.dtype)


def join(x, y, leaves):
    rows, width = x.shape
    half = width // leaves
    if half != 64:
        parts = [p.reshape(rows, leaves, 1, half) for p in (x, y)]
        return jnp.concatenate(parts, axis=2).reshape(rows, 2 * width)
    return pl.pallas_call(
        join_kernel,
        out_shape=jax.ShapeDtypeStruct((rows, 2 * width), x.dtype),
        in_specs=[VMEM, VMEM],
        out_specs=VMEM,
        compiler_params=pltpu.CompilerParams(vmem_limit_bytes=6 << 20),
        name="join",
    )(x, y)


def split_kernel(own, other, *pieces):
    rows = own.shape[0] // 2
    leaf = lax.axis_index("leaf")
    for d, out in enumerate(pieces):
        target = leaf ^ d
        columns = pl.ds(pl.multiple_of((target >> 1) * 128, 128), 128)
        both = own[:, columns] + other[:, columns].astype(F32)
        top, bottom = both[:rows], both[rows:]
        low = low_lanes(top.shape)
        even = jnp.where(low, top, swap_halves(bottom))
        odd = jnp.where(low, swap_halves(top), bottom)
        out[...] = jnp.where((target & 1) == 1, odd, even).astype(out.dtype)


def split(own, other, leaves):
    rows, width = own.shape
    half = width // leaves
    if half != 64:
        leaf = lax.axis_index("leaf")
        q = own + other.astype(F32)
        blocks = [column_block(q, leaf ^ d, half) for d in range(leaves)]
        return blocks[0], *[block.astype(BF16) for block in blocks[1:]]
    return pl.pallas_call(
        split_kernel,
        out_shape=[
            jax.ShapeDtypeStruct((rows // 2, 128), BF16 if d else F32) for d in range(leaves)
        ],
        in_specs=[VMEM, VMEM],
        out_specs=[VMEM] * leaves,
        compiler_params=pltpu.CompilerParams(vmem_limit_bytes=6 << 20),
        name="split",
    )(own, other)


def finish_kernel(n, rhs, *refs):
    groups, out = (refs[:n], refs[n : 2 * n]), refs[2 * n]
    first, second = (sum((g[...].astype(F32) for g in group[1:]), group[0][...]) for group in groups)
    rows = first.shape[0]
    low = low_lanes(first.shape)
    out[:rows] = rhs[:rows] - jnp.where(low, first, swap_halves(second))
    out[rows:] = rhs[rows:] - jnp.where(low, swap_halves(first), second)


def finish(rhs, groups):
    if rhs.shape[1] != 128:
        sums = [sum((g.astype(F32) for g in group[1:]), group[0]) for group in groups]
        return rhs - jnp.concatenate(sums, axis=1)
    n = len(groups[0])
    return pl.pallas_call(
        functools.partial(finish_kernel, n),
        out_shape=jax.ShapeDtypeStruct(rhs.shape, F32),
        in_specs=[VMEM] * (1 + 2 * n),
        out_specs=VMEM,
        compiler_params=pltpu.CompilerParams(vmem_limit_bytes=4 << 20),
        name="finish",
    )(rhs, *groups[0], *groups[1])


def on_device(sep_inverse, rhs_block, coupling, ancestor_rows, ancestor_rhs):
    inverse, rhs, couple = sep_inverse[0], rhs_block[0], coupling[0]
    leaves, n_row = lax.axis_size("leaf"), lax.axis_size("row")
    rows = inverse.shape[0]
    dims = [1 << b for b in range(1, n_row.bit_length() - 1)]
    routes = (dims, dims[::-1])
    masks = ([0], [0])
    for step in range(len(dims)):
        for k in (0, 1):
            masks[k].extend([m ^ routes[k][step] for m in masks[k]])

    def partner(x):
        return lax.ppermute(x, "row", [(i, i ^ 1) for i in range(n_row)])

    def gather(x):
        pieces = [x]
        for step in range(len(dims)):
            pairs = [(i, i ^ routes[i & 1][step]) for i in range(n_row)]
            for p in range(len(pieces)):
                pieces.append(lax.ppermute(pieces[p], "row", pairs))
        return pieces

    gathered = []
    for c in (0, 1):
        x = chunk(rhs, c, leaves)
        gathered.append(gather(x))

    def inv_block(other):
        return pick(masks, other, inverse, rows)

    def cpl_block(other):
        return select_rows(masks, other, couple, ancestor_rows, rows)

    def both(block):
        sent = block(True)
        kept = block(False)
        return kept, partner(sent)

    inv = both(inv_block)
    cpl = both(cpl_block)

    solved = []
    for pieces in gathered:
        own, other = partials(*inv, pieces)
        other = partner(other)
        solved.append((own + other.astype(F32)).astype(BF16))

    groups = []
    for c, y in enumerate(solved):
        pieces = gather(y)
        sums = ()
        if c:
            sums = partials(*cpl, pieces[:-1], other_type=F32)
        first = len(pieces) - 1 if c else 0
        own, other = partials(*cpl, pieces[first:], first, sums)
        other = partner(other)
        group = list(split(own, other, leaves))
        for d in range(1, leaves):
            group[d] = lax.ppermute(group[d], "leaf", [(j, j ^ d) for j in range(leaves)])
        groups.append(group)

    solution = join(*solved, leaves)
    out = finish(ancestor_rhs, groups)
    return (solution[None], out)


def solution(mesh):
    return jax.shard_map(
        on_device,
        mesh=mesh,
        in_specs=(
            P("leaf", "row", None),
            P("leaf", "row", None),
            P("leaf", "row", None),
            P("leaf", "row"),
            P("row", "leaf"),
        ),
        out_specs=(P("leaf", "row", None), P("row", "leaf")),
        check_vma=False,
    )
```

```python
import functools

import jax
import jax.numpy as jnp
from jax import lax
from jax.experimental import pallas as pl
from jax.experimental.pallas import tpu as pltpu
from jax.sharding import PartitionSpec as P

VMEM = pl.BlockSpec(memory_space=pltpu.VMEM)
SPLIT = 2
F32 = jnp.float32
BF16 = jnp.bfloat16


def block_of(masks, other, j):
    me = lax.axis_index("row")
    core = me & 1
    if other:
        me, core = me ^ 1, 1 - core
    return me ^ jnp.where(core == 0, masks[0][j], masks[1][j])


def block_copies(masks, other, src, out, sem):
    n = len(masks[0])
    width = out.shape[1] // n
    rows = out.shape[0] // SPLIT
    copies = []
    for j in range(n):
        start = pl.multiple_of(block_of(masks, other, j) * width, 128)
        copies.append(
            [
                pltpu.make_async_copy(
                    src.at[pl.ds(r * rows, rows), pl.ds(start, width)],
                    out.at[pl.ds(r * rows, rows), pl.ds(j * width, width)],
                    sem.at[j, r],
                )
                for r in range(SPLIT)
            ]
        )
    return copies


def pick_kernel(masks, other, src, out, sem):
    copies = block_copies(masks, other, src, out, sem)
    for group in copies:
        for copy in group:
            copy.start()
    for group in copies:
        for copy in group:
            copy.wait()


def column_block(src, start, width):
    return lax.dynamic_slice_in_dim(src, start * width, width, 1)


def pick(masks, other, src, width):
    n = len(masks[0])
    if width % 128:
        blocks = [column_block(src, block_of(masks, other, j), width) for j in range(n)]
        return jnp.concatenate(blocks, axis=1)
    if other:
        src = pltpu.with_memory_space_constraint(src, pltpu.HBM)
    return pl.pallas_call(
        functools.partial(pick_kernel, masks, other),
        out_shape=jax.ShapeDtypeStruct((src.shape[0], n * width), src.dtype),
        in_specs=[pl.BlockSpec(memory_space=pl.ANY)],
        out_specs=VMEM,
        scratch_shapes=[pltpu.SemaphoreType.DMA((n, SPLIT))],
        compiler_params=pltpu.CompilerParams(vmem_limit_bytes=8 << 20),
        name="pick",
    )(src)


def one_hot(places, rows):
    first = lax.axis_index("row") * rows
    return lax.broadcasted_iota(jnp.int32, (rows, rows), 0) + first == places


def select_kernel(masks, other, places, src, out, buf, sem):
    rows, n = buf.shape[0], len(masks[0])
    width = buf.shape[1] // n
    copies = block_copies(masks, other, src, buf, sem)
    for group in copies:
        for copy in group:
            copy.start()
    hot = jnp.where(one_hot(places[...], rows), 1.0, 0.0).astype(BF16)
    for j, group in enumerate(copies):
        for copy in group:
            copy.wait()
        block = slice(j * width, (j + 1) * width)
        out[:, block] = jnp.dot(hot, buf[:, block], preferred_element_type=F32).astype(BF16)


def select_rows(masks, other, src, places, width):
    rows, n = src.shape[0], len(masks[0])
    if width % 128:
        return one_hot(places, rows).astype(src.dtype) @ pick(masks, other, src, width)
    return pl.pallas_call(
        functools.partial(select_kernel, masks, other),
        out_shape=jax.ShapeDtypeStruct((rows, n * width), src.dtype),
        in_specs=[VMEM, pl.BlockSpec(memory_space=pl.ANY)],
        out_specs=VMEM,
        scratch_shapes=[
            pltpu.VMEM((rows, n * width), src.dtype),
            pltpu.SemaphoreType.DMA((n, SPLIT)),
        ],
        compiler_params=pltpu.CompilerParams(vmem_limit_bytes=12 << 20),
        name="select_rows",
    )(places, src)


def partial_kernel(n, first, had, keep, swap, *refs):
    pieces, sums, (own, other, joined) = refs[:n], refs[n : n + 2 * had], refs[n + 2 * had :]
    depth = pieces[0].shape[0]
    for j in range(n):
        joined[j * depth : (j + 1) * depth, :] = pieces[j][...]
    columns = slice(first * depth, (first + n) * depth)
    for k, (block, out) in enumerate(((keep, own), (swap, other))):
        value = jnp.dot(block[:, columns], joined[...], preferred_element_type=F32)
        if had:
            value = value + sums[k][...]
        out[...] = value.astype(out.dtype)


def partials(keep, swap, pieces, first=0, sums=(), other_type=BF16):
    n = len(pieces)
    rows = keep.shape[0]
    depth, width = pieces[0].shape
    return pl.pallas_call(
        functools.partial(partial_kernel, n, first, bool(sums)),
        out_shape=(
            jax.ShapeDtypeStruct((rows, width), F32),
            jax.ShapeDtypeStruct((rows, width), other_type),
        ),
        in_specs=[VMEM] * (2 + n + len(sums)),
        out_specs=(VMEM, VMEM),
        scratch_shapes=[pltpu.VMEM((n * depth, width), BF16)],
        compiler_params=pltpu.CompilerParams(vmem_limit_bytes=12 << 20),
        name="partials",
    )(keep, swap, *pieces, *sums)


def swap_halves(x):
    return pltpu.roll(x, x.shape[1] // 2, 1)


def low_lanes(shape):
    return lax.broadcasted_iota(jnp.int32, shape, 1) < shape[1] // 2


def tile(t):
    return slice(t * 128, (t + 1) * 128)


def halves(c, x, out):
    for t in range(out.shape[1] // 128):
        a, b = x[:, tile(2 * t)].astype(F32), x[:, tile(2 * t + 1)].astype(F32)
        low = low_lanes(a.shape)
        both = jnp.where(low, swap_halves(a), b) if c else jnp.where(low, a, swap_halves(b))
        out[:, tile(t)] = both.astype(out.dtype)


def chunk_kernel(c, x, out, buf, sem):
    rows = x.shape[0] // SPLIT
    copies = [
        pltpu.make_async_copy(
            x.at[pl.ds(r * rows, rows)], buf.at[pl.ds(r * rows, rows)], sem.at[r]
        )
        for r in range(SPLIT)
    ]
    for copy in copies:
        copy.start()
    for r, copy in enumerate(copies):
        copy.wait()
        block = pl.ds(r * rows, rows)
        halves(c, buf.at[block], out.at[block])


def chunk(x, c, leaves):
    rows, width = x.shape
    half = width // leaves // 2
    if half != 64:
        return x.reshape(rows, leaves, 2, half)[:, :, c].reshape(rows, width // 2)
    out = jax.ShapeDtypeStruct((rows, width // 2), x.dtype)
    if c:
        return pl.pallas_call(
            functools.partial(halves, c),
            out_shape=out,
            in_specs=[VMEM],
            out_specs=VMEM,
            compiler_params=pltpu.CompilerParams(vmem_limit_bytes=4 << 20),
            name="chunk",
        )(x)
    return pl.pallas_call(
        functools.partial(chunk_kernel, c),
        out_shape=out,
        in_specs=[pl.BlockSpec(memory_space=pl.ANY)],
        out_specs=VMEM,
        scratch_shapes=[pltpu.VMEM((rows, width), x.dtype), pltpu.SemaphoreType.DMA((SPLIT,))],
        compiler_params=pltpu.CompilerParams(vmem_limit_bytes=4 << 20),
        name="chunk",
    )(pltpu.with_memory_space_constraint(x, pltpu.HBM))


def join_kernel(x, y, out):
    for t in range(x.shape[1] // 128):
        a, b = x[:, tile(t)].astype(F32), y[:, tile(t)].astype(F32)
        low = low_lanes(a.shape)
        out[:, tile(2 * t)] = jnp.where(low, a, swap_halves(b)).astype(out.dtype)
        out[:, tile(2 * t + 1)] = jnp.where(low, swap_halves(a), b).astype(out.dtype)


def join(x, y, leaves):
    rows, width = x.shape
    half = width // leaves
    if half != 64:
        parts = [p.reshape(rows, leaves, 1, half) for p in (x, y)]
        return jnp.concatenate(parts, axis=2).reshape(rows, 2 * width)
    return pl.pallas_call(
        join_kernel,
        out_shape=jax.ShapeDtypeStruct((rows, 2 * width), x.dtype),
        in_specs=[VMEM, VMEM],
        out_specs=VMEM,
        compiler_params=pltpu.CompilerParams(vmem_limit_bytes=6 << 20),
        name="join",
    )(x, y)


def split_kernel(own, other, *pieces):
    rows = own.shape[0] // 2
    leaf = lax.axis_index("leaf")
    for d, out in enumerate(pieces):
        target = leaf ^ d
        columns = pl.ds(pl.multiple_of((target >> 1) * 128, 128), 128)
        both = own[:, columns] + other[:, columns].astype(F32)
        top, bottom = both[:rows], both[rows:]
        low = low_lanes(top.shape)
        even = jnp.where(low, top, swap_halves(bottom))
        odd = jnp.where(low, swap_halves(top), bottom)
        out[...] = jnp.where((target & 1) == 1, odd, even).astype(out.dtype)


def split(own, other, leaves):
    rows, width = own.shape
    half = width // leaves
    if half != 64:
        leaf = lax.axis_index("leaf")
        q = own + other.astype(F32)
        blocks = [column_block(q, leaf ^ d, half) for d in range(leaves)]
        return blocks[0], *[block.astype(BF16) for block in blocks[1:]]
    return pl.pallas_call(
        split_kernel,
        out_shape=[
            jax.ShapeDtypeStruct((rows // 2, 128), BF16 if d else F32) for d in range(leaves)
        ],
        in_specs=[VMEM, VMEM],
        out_specs=[VMEM] * leaves,
        compiler_params=pltpu.CompilerParams(vmem_limit_bytes=6 << 20),
        name="split",
    )(own, other)


def finish_kernel(n, rhs, *refs):
    groups, out = (refs[:n], refs[n : 2 * n]), refs[2 * n]
    first, second = (sum((g[...].astype(F32) for g in group[1:]), group[0][...]) for group in groups)
    rows = first.shape[0]
    low = low_lanes(first.shape)
    out[:rows] = rhs[:rows] - jnp.where(low, first, swap_halves(second))
    out[rows:] = rhs[rows:] - jnp.where(low, swap_halves(first), second)


def finish(rhs, groups):
    if rhs.shape[1] != 128:
        sums = [sum((g.astype(F32) for g in group[1:]), group[0]) for group in groups]
        return rhs - jnp.concatenate(sums, axis=1)
    n = len(groups[0])
    return pl.pallas_call(
        functools.partial(finish_kernel, n),
        out_shape=jax.ShapeDtypeStruct(rhs.shape, F32),
        in_specs=[VMEM] * (1 + 2 * n),
        out_specs=VMEM,
        compiler_params=pltpu.CompilerParams(vmem_limit_bytes=4 << 20),
        name="finish",
    )(rhs, *groups[0], *groups[1])


def on_device(sep_inverse, rhs_block, coupling, ancestor_rows, ancestor_rhs):
    inverse, rhs, couple = sep_inverse[0], rhs_block[0], coupling[0]
    leaves, n_row = lax.axis_size("leaf"), lax.axis_size("row")
    rows = inverse.shape[0]
    dims = [1 << b for b in range(1, n_row.bit_length() - 1)]
    routes = (dims, dims[::-1])
    masks = ([0], [0])
    for step in range(len(dims)):
        for k in (0, 1):
            masks[k].extend([m ^ routes[k][step] for m in masks[k]])

    def partner(x):
        return lax.ppermute(x, "row", [(i, i ^ 1) for i in range(n_row)])

    def gather(x):
        pieces = [x]
        for step in range(len(dims)):
            pairs = [(i, i ^ routes[i & 1][step]) for i in range(n_row)]
            for p in range(len(pieces)):
                pieces.append(lax.ppermute(pieces[p], "row", pairs))
        return pieces

    gathered = []
    for c in (0, 1):
        x = chunk(rhs, c, leaves)
        gathered.append(gather(x))

    def inv_block(other):
        return pick(masks, other, inverse, rows)

    def cpl_block(other):
        return select_rows(masks, other, couple, ancestor_rows, rows)

    def both(block):
        sent = block(True)
        kept = block(False)
        return kept, partner(sent)

    inv = both(inv_block)
    cpl = both(cpl_block)

    solved = []
    for pieces in gathered:
        own, other = partials(*inv, pieces)
        other = partner(other)
        solved.append((own + other.astype(F32)).astype(BF16))

    groups = []
    for c, y in enumerate(solved):
        pieces = gather(y)
        sums = ()
        if c:
            sums = partials(*cpl, pieces[:-1], other_type=F32)
        first = len(pieces) - 1 if c else 0
        own, other = partials(*cpl, pieces[first:], first, sums)
        other = partner(other)
        group = list(split(own, other, leaves))
        for d in range(1, leaves):
            group[d] = lax.ppermute(group[d], "leaf", [(j, j ^ d) for j in range(leaves)])
        groups.append(group)

    solution = join(*solved, leaves)
    out = finish(ancestor_rhs, groups)
    return (solution[None], out)


def solution(mesh):
    return jax.shard_map(
        on_device,
        mesh=mesh,
        in_specs=(
            P("leaf", "row", None),
            P("leaf", "row", None),
            P("leaf", "row", None),
            P("leaf", "row"),
            P("row", "leaf"),
        ),
        out_specs=(P("leaf", "row", None), P("row", "leaf")),
        check_vma=False,
    )
```

```python
import functools

import jax
import jax.numpy as jnp
from jax import lax
from jax.experimental import pallas as pl
from jax.experimental.pallas import tpu as pltpu
from jax.sharding import PartitionSpec as P

VMEM = pl.BlockSpec(memory_space=pltpu.VMEM)
SPLIT = 2
F32 = jnp.float32
BF16 = jnp.bfloat16


def block_of(masks, other, j):
    me = lax.axis_index("row")
    core = me & 1
    if other:
        me, core = me ^ 1, 1 - core
    return me ^ jnp.where(core == 0, masks[0][j], masks[1][j])


def block_copies(masks, other, src, out, sem):
    n = len(masks[0])
    width = out.shape[1] // n
    rows = out.shape[0] // SPLIT
    copies = []
    for j in range(n):
        start = pl.multiple_of(block_of(masks, other, j) * width, 128)
        copies.append(
            [
                pltpu.make_async_copy(
                    src.at[pl.ds(r * rows, rows), pl.ds(start, width)],
                    out.at[pl.ds(r * rows, rows), pl.ds(j * width, width)],
                    sem.at[j, r],
                )
                for r in range(SPLIT)
            ]
        )
    return copies


def pick_kernel(masks, other, src, out, sem):
    copies = block_copies(masks, other, src, out, sem)
    for group in copies:
        for copy in group:
            copy.start()
    for group in copies:
        for copy in group:
            copy.wait()


def column_block(src, start, width):
    return lax.dynamic_slice_in_dim(src, start * width, width, 1)


def pick(masks, other, src, width):
    n = len(masks[0])
    if width % 128:
        blocks = [column_block(src, block_of(masks, other, j), width) for j in range(n)]
        return jnp.concatenate(blocks, axis=1)
    if other:
        src = pltpu.with_memory_space_constraint(src, pltpu.HBM)
    return pl.pallas_call(
        functools.partial(pick_kernel, masks, other),
        out_shape=jax.ShapeDtypeStruct((src.shape[0], n * width), src.dtype),
        in_specs=[pl.BlockSpec(memory_space=pl.ANY)],
        out_specs=VMEM,
        scratch_shapes=[pltpu.SemaphoreType.DMA((n, SPLIT))],
        compiler_params=pltpu.CompilerParams(vmem_limit_bytes=8 << 20),
        name="pick",
    )(src)


def one_hot(places, rows):
    first = lax.axis_index("row") * rows
    return lax.broadcasted_iota(jnp.int32, (rows, rows), 0) + first == places


def select_kernel(masks, other, places, src, out, buf, sem):
    rows, n = buf.shape[0], len(masks[0])
    width = buf.shape[1] // n
    copies = block_copies(masks, other, src, buf, sem)
    for group in copies:
        for copy in group:
            copy.start()
    hot = jnp.where(one_hot(places[...], rows), 1.0, 0.0).astype(BF16)
    for j, group in enumerate(copies):
        for copy in group:
            copy.wait()
        block = slice(j * width, (j + 1) * width)
        out[:, block] = jnp.dot(hot, buf[:, block], preferred_element_type=F32).astype(BF16)


def select_rows(masks, other, src, places, width):
    rows, n = src.shape[0], len(masks[0])
    if width % 128:
        return one_hot(places, rows).astype(src.dtype) @ pick(masks, other, src, width)
    return pl.pallas_call(
        functools.partial(select_kernel, masks, other),
        out_shape=jax.ShapeDtypeStruct((rows, n * width), src.dtype),
        in_specs=[VMEM, pl.BlockSpec(memory_space=pl.ANY)],
        out_specs=VMEM,
        scratch_shapes=[
            pltpu.VMEM((rows, n * width), src.dtype),
            pltpu.SemaphoreType.DMA((n, SPLIT)),
        ],
        compiler_params=pltpu.CompilerParams(vmem_limit_bytes=12 << 20),
        name="select_rows",
    )(places, src)


def partial_kernel(n, first, had, keep, swap, *refs):
    pieces, sums, (own, other, joined) = refs[:n], refs[n : n + 2 * had], refs[n + 2 * had :]
    depth = pieces[0].shape[0]
    for j in range(n):
        joined[j * depth : (j + 1) * depth, :] = pieces[j][...]
    columns = slice(first * depth, (first + n) * depth)
    for k, (block, out) in enumerate(((keep, own), (swap, other))):
        value = jnp.dot(block[:, columns], joined[...], preferred_element_type=F32)
        if had:
            value = value + sums[k][...]
        out[...] = value.astype(out.dtype)


def partials(keep, swap, pieces, first=0, sums=(), other_type=BF16):
    n = len(pieces)
    rows = keep.shape[0]
    depth, width = pieces[0].shape
    return pl.pallas_call(
        functools.partial(partial_kernel, n, first, bool(sums)),
        out_shape=(
            jax.ShapeDtypeStruct((rows, width), F32),
            jax.ShapeDtypeStruct((rows, width), other_type),
        ),
        in_specs=[VMEM] * (2 + n + len(sums)),
        out_specs=(VMEM, VMEM),
        scratch_shapes=[pltpu.VMEM((n * depth, width), BF16)],
        compiler_params=pltpu.CompilerParams(vmem_limit_bytes=12 << 20),
        name="partials",
    )(keep, swap, *pieces, *sums)


def swap_halves(x):
    return pltpu.roll(x, x.shape[1] // 2, 1)


def last_kernel(column, block, piece, early, out):
    depth = piece.shape[0]
    value = jnp.dot(block[:, column : column + depth], piece[...], preferred_element_type=F32)
    out[...] = (early[...] + value).astype(out.dtype)


def last_part(block, piece, early, place, kind):
    return pl.pallas_call(
        functools.partial(last_kernel, place * piece.shape[0]),
        out_shape=jax.ShapeDtypeStruct(early.shape, kind),
        in_specs=[VMEM] * 3,
        out_specs=VMEM,
        compiler_params=pltpu.CompilerParams(vmem_limit_bytes=8 << 20),
        name="last_part",
    )(block, piece, early)


def low_lanes(shape):
    return lax.broadcasted_iota(jnp.int32, shape, 1) < shape[1] // 2


def tile(t):
    return slice(t * 128, (t + 1) * 128)


def halves(c, x, out):
    for t in range(out.shape[1] // 128):
        a, b = x[:, tile(2 * t)].astype(F32), x[:, tile(2 * t + 1)].astype(F32)
        low = low_lanes(a.shape)
        both = jnp.where(low, swap_halves(a), b) if c else jnp.where(low, a, swap_halves(b))
        out[:, tile(t)] = both.astype(out.dtype)


def chunk_kernel(c, x, out, buf, sem):
    rows = x.shape[0] // SPLIT
    copies = [
        pltpu.make_async_copy(
            x.at[pl.ds(r * rows, rows)], buf.at[pl.ds(r * rows, rows)], sem.at[r]
        )
        for r in range(SPLIT)
    ]
    for copy in copies:
        copy.start()
    for r, copy in enumerate(copies):
        copy.wait()
        block = pl.ds(r * rows, rows)
        halves(c, buf.at[block], out.at[block])


def chunk(x, c, leaves):
    rows, width = x.shape
    half = width // leaves // 2
    if half != 64:
        return x.reshape(rows, leaves, 2, half)[:, :, c].reshape(rows, width // 2)
    out = jax.ShapeDtypeStruct((rows, width // 2), x.dtype)
    if c:
        return pl.pallas_call(
            functools.partial(halves, c),
            out_shape=out,
            in_specs=[VMEM],
            out_specs=VMEM,
            compiler_params=pltpu.CompilerParams(vmem_limit_bytes=4 << 20),
            name="chunk",
        )(x)
    return pl.pallas_call(
        functools.partial(chunk_kernel, c),
        out_shape=out,
        in_specs=[pl.BlockSpec(memory_space=pl.ANY)],
        out_specs=VMEM,
        scratch_shapes=[pltpu.VMEM((rows, width), x.dtype), pltpu.SemaphoreType.DMA((SPLIT,))],
        compiler_params=pltpu.CompilerParams(vmem_limit_bytes=4 << 20),
        name="chunk",
    )(pltpu.with_memory_space_constraint(x, pltpu.HBM))


def join_kernel(x, y, out):
    for t in range(x.shape[1] // 128):
        a, b = x[:, tile(t)].astype(F32), y[:, tile(t)].astype(F32)
        low = low_lanes(a.shape)
        out[:, tile(2 * t)] = jnp.where(low, a, swap_halves(b)).astype(out.dtype)
        out[:, tile(2 * t + 1)] = jnp.where(low, swap_halves(a), b).astype(out.dtype)


def join(x, y, leaves):
    rows, width = x.shape
    half = width // leaves
    if half != 64:
        parts = [p.reshape(rows, leaves, 1, half) for p in (x, y)]
        return jnp.concatenate(parts, axis=2).reshape(rows, 2 * width)
    return pl.pallas_call(
        join_kernel,
        out_shape=jax.ShapeDtypeStruct((rows, 2 * width), x.dtype),
        in_specs=[VMEM, VMEM],
        out_specs=VMEM,
        compiler_params=pltpu.CompilerParams(vmem_limit_bytes=6 << 20),
        name="join",
    )(x, y)


def split_kernel(own, other, *pieces):
    rows = own.shape[0] // 2
    leaf = lax.axis_index("leaf")
    for d, out in enumerate(pieces):
        target = leaf ^ d
        columns = pl.ds(pl.multiple_of((target >> 1) * 128, 128), 128)
        both = own[:, columns] + other[:, columns].astype(F32)
        top, bottom = both[:rows], both[rows:]
        low = low_lanes(top.shape)
        even = jnp.where(low, top, swap_halves(bottom))
        odd = jnp.where(low, swap_halves(top), bottom)
        out[...] = jnp.where((target & 1) == 1, odd, even).astype(out.dtype)


def split(own, other, leaves):
    rows, width = own.shape
    half = width // leaves
    if half != 64:
        leaf = lax.axis_index("leaf")
        q = own + other.astype(F32)
        blocks = [column_block(q, leaf ^ d, half) for d in range(leaves)]
        return blocks[0], *[block.astype(BF16) for block in blocks[1:]]
    return pl.pallas_call(
        split_kernel,
        out_shape=[
            jax.ShapeDtypeStruct((rows // 2, 128), BF16 if d else F32) for d in range(leaves)
        ],
        in_specs=[VMEM, VMEM],
        out_specs=[VMEM] * leaves,
        compiler_params=pltpu.CompilerParams(vmem_limit_bytes=6 << 20),
        name="split",
    )(own, other)


def finish_kernel(n, rhs, *refs):
    groups, out = (refs[:n], refs[n : 2 * n]), refs[2 * n]
    first, second = (sum((g[...].astype(F32) for g in group[1:]), group[0][...]) for group in groups)
    rows = first.shape[0]
    low = low_lanes(first.shape)
    out[:rows] = rhs[:rows] - jnp.where(low, first, swap_halves(second))
    out[rows:] = rhs[rows:] - jnp.where(low, swap_halves(first), second)


def finish(rhs, groups):
    if rhs.shape[1] != 128:
        sums = [sum((g.astype(F32) for g in group[1:]), group[0]) for group in groups]
        return rhs - jnp.concatenate(sums, axis=1)
    n = len(groups[0])
    return pl.pallas_call(
        functools.partial(finish_kernel, n),
        out_shape=jax.ShapeDtypeStruct(rhs.shape, F32),
        in_specs=[VMEM] * (1 + 2 * n),
        out_specs=VMEM,
        compiler_params=pltpu.CompilerParams(vmem_limit_bytes=4 << 20),
        name="finish",
    )(rhs, *groups[0], *groups[1])


def on_device(sep_inverse, rhs_block, coupling, ancestor_rows, ancestor_rhs):
    inverse, rhs, couple = sep_inverse[0], rhs_block[0], coupling[0]
    leaves, n_row = lax.axis_size("leaf"), lax.axis_size("row")
    rows = inverse.shape[0]
    dims = [1 << b for b in range(1, n_row.bit_length() - 1)]
    routes = (dims, dims[::-1])
    masks = ([0], [0])
    for step in range(len(dims)):
        for k in (0, 1):
            masks[k].extend([m ^ routes[k][step] for m in masks[k]])

    def partner(x):
        return lax.ppermute(x, "row", [(i, i ^ 1) for i in range(n_row)])

    def gather(x):
        pieces = [x]
        for step in range(len(dims)):
            pairs = [(i, i ^ routes[i & 1][step]) for i in range(n_row)]
            for p in range(len(pieces)):
                pieces.append(lax.ppermute(pieces[p], "row", pairs))
        return pieces

    gathered = []
    for c in (0, 1):
        x = chunk(rhs, c, leaves)
        gathered.append(gather(x))

    def inv_block(other):
        return pick(masks, other, inverse, rows)

    def cpl_block(other):
        return select_rows(masks, other, couple, ancestor_rows, rows)

    def both(block):
        sent = block(True)
        kept = block(False)
        return kept, partner(sent)

    inv = both(inv_block)
    cpl = both(cpl_block)

    solved = []
    for pieces in gathered:
        own, other = partials(*inv, pieces)
        other = partner(other)
        solved.append((own + other.astype(F32)).astype(BF16))

    groups = []
    for c, y in enumerate(solved):
        pieces = gather(y)
        if c:
            own, other = partials(*cpl, pieces[:-1], other_type=F32)
            place = len(pieces) - 1
            other = last_part(cpl[1], pieces[-1], other, place, BF16)
            own = last_part(cpl[0], pieces[-1], own, place, F32)
        else:
            own, other = partials(*cpl, pieces)
        other = partner(other)
        group = list(split(own, other, leaves))
        for d in range(1, leaves):
            group[d] = lax.ppermute(group[d], "leaf", [(j, j ^ d) for j in range(leaves)])
        groups.append(group)

    solution = join(*solved, leaves)
    out = finish(ancestor_rhs, groups)
    return (solution[None], out)


def solution(mesh):
    return jax.shard_map(
        on_device,
        mesh=mesh,
        in_specs=(
            P("leaf", "row", None),
            P("leaf", "row", None),
            P("leaf", "row", None),
            P("leaf", "row"),
            P("row", "leaf"),
        ),
        out_specs=(P("leaf", "row", None), P("row", "leaf")),
        check_vma=False,
    )
```

```python
import functools

import jax
import jax.numpy as jnp
from jax import lax
from jax.experimental import pallas as pl
from jax.experimental.pallas import tpu as pltpu
from jax.sharding import PartitionSpec as P

VMEM = pl.BlockSpec(memory_space=pltpu.VMEM)
SPLIT = 2
F32 = jnp.float32
BF16 = jnp.bfloat16


def block_of(masks, other, j):
    me = lax.axis_index("row")
    core = me & 1
    if other:
        me, core = me ^ 1, 1 - core
    return me ^ jnp.where(core == 0, masks[0][j], masks[1][j])


def block_copies(masks, other, src, out, sem):
    n = len(masks[0])
    width = out.shape[1] // n
    rows = out.shape[0] // SPLIT
    copies = []
    for j in range(n):
        start = pl.multiple_of(block_of(masks, other, j) * width, 128)
        copies.append(
            [
                pltpu.make_async_copy(
                    src.at[pl.ds(r * rows, rows), pl.ds(start, width)],
                    out.at[pl.ds(r * rows, rows), pl.ds(j * width, width)],
                    sem.at[j, r],
                )
                for r in range(SPLIT)
            ]
        )
    return copies


def pick_kernel(masks, other, src, out, sem):
    copies = block_copies(masks, other, src, out, sem)
    for group in copies:
        for copy in group:
            copy.start()
    for group in copies:
        for copy in group:
            copy.wait()


def column_block(src, start, width):
    return lax.dynamic_slice_in_dim(src, start * width, width, 1)


def pick(masks, other, src, width):
    n = len(masks[0])
    if width % 128:
        blocks = [column_block(src, block_of(masks, other, j), width) for j in range(n)]
        return jnp.concatenate(blocks, axis=1)
    if other:
        src = pltpu.with_memory_space_constraint(src, pltpu.HBM)
    return pl.pallas_call(
        functools.partial(pick_kernel, masks, other),
        out_shape=jax.ShapeDtypeStruct((src.shape[0], n * width), src.dtype),
        in_specs=[pl.BlockSpec(memory_space=pl.ANY)],
        out_specs=VMEM,
        scratch_shapes=[pltpu.SemaphoreType.DMA((n, SPLIT))],
        compiler_params=pltpu.CompilerParams(vmem_limit_bytes=8 << 20),
        name="pick",
    )(src)


def one_hot(places, rows):
    first = lax.axis_index("row") * rows
    return lax.broadcasted_iota(jnp.int32, (rows, rows), 0) + first == places


def select_kernel(masks, other, places, src, out, buf, sem):
    rows, n = buf.shape[0], len(masks[0])
    width = buf.shape[1] // n
    copies = block_copies(masks, other, src, buf, sem)
    for group in copies:
        for copy in group:
            copy.start()
    hot = jnp.where(one_hot(places[...], rows), 1.0, 0.0).astype(BF16)
    for j, group in enumerate(copies):
        for copy in group:
            copy.wait()
        block = slice(j * width, (j + 1) * width)
        out[:, block] = jnp.dot(hot, buf[:, block], preferred_element_type=F32).astype(BF16)


def select_rows(masks, other, src, places, width):
    rows, n = src.shape[0], len(masks[0])
    if width % 128:
        return one_hot(places, rows).astype(src.dtype) @ pick(masks, other, src, width)
    return pl.pallas_call(
        functools.partial(select_kernel, masks, other),
        out_shape=jax.ShapeDtypeStruct((rows, n * width), src.dtype),
        in_specs=[VMEM, pl.BlockSpec(memory_space=pl.ANY)],
        out_specs=VMEM,
        scratch_shapes=[
            pltpu.VMEM((rows, n * width), src.dtype),
            pltpu.SemaphoreType.DMA((n, SPLIT)),
        ],
        compiler_params=pltpu.CompilerParams(vmem_limit_bytes=12 << 20),
        name="select_rows",
    )(places, src)


def partial_kernel(n, first, had, keep, swap, *refs):
    pieces, sums, (own, other, joined) = refs[:n], refs[n : n + 2 * had], refs[n + 2 * had :]
    depth = pieces[0].shape[0]
    for j in range(n):
        joined[j * depth : (j + 1) * depth, :] = pieces[j][...]
    columns = slice(first * depth, (first + n) * depth)
    for k, (block, out) in enumerate(((keep, own), (swap, other))):
        value = jnp.dot(block[:, columns], joined[...], preferred_element_type=F32)
        if had:
            value = value + sums[k][...]
        out[...] = value.astype(out.dtype)


def partials(keep, swap, pieces, first=0, sums=(), other_type=BF16):
    n = len(pieces)
    rows = keep.shape[0]
    depth, width = pieces[0].shape
    return pl.pallas_call(
        functools.partial(partial_kernel, n, first, bool(sums)),
        out_shape=(
            jax.ShapeDtypeStruct((rows, width), F32),
            jax.ShapeDtypeStruct((rows, width), other_type),
        ),
        in_specs=[VMEM] * (2 + n + len(sums)),
        out_specs=(VMEM, VMEM),
        scratch_shapes=[pltpu.VMEM((n * depth, width), BF16)],
        compiler_params=pltpu.CompilerParams(vmem_limit_bytes=12 << 20),
        name="partials",
    )(keep, swap, *pieces, *sums)


def swap_halves(x):
    return pltpu.roll(x, x.shape[1] // 2, 1)


def last_kernel(column, block, piece, early, out):
    depth = piece.shape[0]
    value = jnp.dot(block[:, column : column + depth], piece[...], preferred_element_type=F32)
    out[...] = (early[...] + value).astype(out.dtype)


def last_part(block, piece, early, place, kind):
    return pl.pallas_call(
        functools.partial(last_kernel, place * piece.shape[0]),
        out_shape=jax.ShapeDtypeStruct(early.shape, kind),
        in_specs=[VMEM] * 3,
        out_specs=VMEM,
        compiler_params=pltpu.CompilerParams(vmem_limit_bytes=8 << 20),
        name="last_part",
    )(block, piece, early)


def low_lanes(shape):
    return lax.broadcasted_iota(jnp.int32, shape, 1) < shape[1] // 2


def tile(t):
    return slice(t * 128, (t + 1) * 128)


def halves(c, x, out):
    for t in range(out.shape[1] // 128):
        a, b = x[:, tile(2 * t)].astype(F32), x[:, tile(2 * t + 1)].astype(F32)
        low = low_lanes(a.shape)
        both = jnp.where(low, swap_halves(a), b) if c else jnp.where(low, a, swap_halves(b))
        out[:, tile(t)] = both.astype(out.dtype)


def chunk_kernel(c, x, out, buf, sem):
    rows = x.shape[0] // SPLIT
    copies = [
        pltpu.make_async_copy(
            x.at[pl.ds(r * rows, rows)], buf.at[pl.ds(r * rows, rows)], sem.at[r]
        )
        for r in range(SPLIT)
    ]
    for copy in copies:
        copy.start()
    for r, copy in enumerate(copies):
        copy.wait()
        block = pl.ds(r * rows, rows)
        halves(c, buf.at[block], out.at[block])


def chunk(x, c, leaves):
    rows, width = x.shape
    half = width // leaves // 2
    if half != 64:
        return x.reshape(rows, leaves, 2, half)[:, :, c].reshape(rows, width // 2)
    out = jax.ShapeDtypeStruct((rows, width // 2), x.dtype)
    if c:
        return pl.pallas_call(
            functools.partial(halves, c),
            out_shape=out,
            in_specs=[VMEM],
            out_specs=VMEM,
            compiler_params=pltpu.CompilerParams(vmem_limit_bytes=4 << 20),
            name="chunk",
        )(x)
    return pl.pallas_call(
        functools.partial(chunk_kernel, c),
        out_shape=out,
        in_specs=[pl.BlockSpec(memory_space=pl.ANY)],
        out_specs=VMEM,
        scratch_shapes=[pltpu.VMEM((rows, width), x.dtype), pltpu.SemaphoreType.DMA((SPLIT,))],
        compiler_params=pltpu.CompilerParams(vmem_limit_bytes=4 << 20),
        name="chunk",
    )(pltpu.with_memory_space_constraint(x, pltpu.HBM))


def join_kernel(x, y, out):
    for t in range(x.shape[1] // 128):
        a, b = x[:, tile(t)].astype(F32), y[:, tile(t)].astype(F32)
        low = low_lanes(a.shape)
        out[:, tile(2 * t)] = jnp.where(low, a, swap_halves(b)).astype(out.dtype)
        out[:, tile(2 * t + 1)] = jnp.where(low, swap_halves(a), b).astype(out.dtype)


def join(x, y, leaves):
    rows, width = x.shape
    half = width // leaves
    if half != 64:
        parts = [p.reshape(rows, leaves, 1, half) for p in (x, y)]
        return jnp.concatenate(parts, axis=2).reshape(rows, 2 * width)
    return pl.pallas_call(
        join_kernel,
        out_shape=jax.ShapeDtypeStruct((rows, 2 * width), x.dtype),
        in_specs=[VMEM, VMEM],
        out_specs=VMEM,
        compiler_params=pltpu.CompilerParams(vmem_limit_bytes=6 << 20),
        name="join",
    )(x, y)


def split_kernel(own, other, *pieces):
    rows = own.shape[0] // 2
    leaf = lax.axis_index("leaf")
    for d, out in enumerate(pieces):
        target = leaf ^ d
        columns = pl.ds(pl.multiple_of((target >> 1) * 128, 128), 128)
        both = own[:, columns] + other[:, columns].astype(F32)
        top, bottom = both[:rows], both[rows:]
        low = low_lanes(top.shape)
        even = jnp.where(low, top, swap_halves(bottom))
        odd = jnp.where(low, swap_halves(top), bottom)
        out[...] = jnp.where((target & 1) == 1, odd, even).astype(out.dtype)


def split(own, other, leaves):
    rows, width = own.shape
    half = width // leaves
    if half != 64:
        leaf = lax.axis_index("leaf")
        q = own + other.astype(F32)
        blocks = [column_block(q, leaf ^ d, half) for d in range(leaves)]
        return blocks[0], *[block.astype(BF16) for block in blocks[1:]]
    return pl.pallas_call(
        split_kernel,
        out_shape=[
            jax.ShapeDtypeStruct((rows // 2, 128), BF16 if d else F32) for d in range(leaves)
        ],
        in_specs=[VMEM, VMEM],
        out_specs=[VMEM] * leaves,
        compiler_params=pltpu.CompilerParams(vmem_limit_bytes=6 << 20),
        name="split",
    )(own, other)


def finish_kernel(n, rhs, *refs):
    groups, out = (refs[:n], refs[n:-1]), refs[-1]
    first, second = (
        sum((g[...].astype(F32) for g in group[1:]), group[0][...]) for group in groups
    )
    rows = first.shape[0]
    low = low_lanes(first.shape)
    out[:rows] = rhs[:rows] - jnp.where(low, first, swap_halves(second))
    out[rows:] = rhs[rows:] - jnp.where(low, swap_halves(first), second)


def finish(rhs, groups):
    if rhs.shape[1] != 128:
        sums = [sum((g.astype(F32) for g in group[1:]), group[0]) for group in groups]
        return rhs - jnp.concatenate(sums, axis=1)
    n = len(groups[0])
    return pl.pallas_call(
        functools.partial(finish_kernel, n),
        out_shape=jax.ShapeDtypeStruct(rhs.shape, F32),
        in_specs=[VMEM] * (1 + n + len(groups[1])),
        out_specs=VMEM,
        compiler_params=pltpu.CompilerParams(vmem_limit_bytes=4 << 20),
        name="finish",
    )(rhs, *groups[0], *groups[1])


def on_device(sep_inverse, rhs_block, coupling, ancestor_rows, ancestor_rhs):
    inverse, rhs, couple = sep_inverse[0], rhs_block[0], coupling[0]
    leaves, n_row = lax.axis_size("leaf"), lax.axis_size("row")
    rows = inverse.shape[0]
    dims = [1 << b for b in range(1, n_row.bit_length() - 1)]
    routes = (dims, dims[::-1])
    masks = ([0], [0])
    for step in range(len(dims)):
        for k in (0, 1):
            masks[k].extend([m ^ routes[k][step] for m in masks[k]])

    def partner(x):
        return lax.ppermute(x, "row", [(i, i ^ 1) for i in range(n_row)])

    def gather(x):
        pieces = [x]
        for step in range(len(dims)):
            pairs = [(i, i ^ routes[i & 1][step]) for i in range(n_row)]
            for p in range(len(pieces)):
                pieces.append(lax.ppermute(pieces[p], "row", pairs))
        return pieces

    gathered = []
    for c in (0, 1):
        x = chunk(rhs, c, leaves)
        gathered.append(gather(x))

    def inv_block(other):
        return pick(masks, other, inverse, rows)

    def cpl_block(other):
        return select_rows(masks, other, couple, ancestor_rows, rows)

    def both(block):
        sent = block(True)
        kept = block(False)
        return kept, partner(sent)

    inv = both(inv_block)
    cpl = both(cpl_block)

    solved = []
    for pieces in gathered:
        own, other = partials(*inv, pieces)
        other = partner(other)
        solved.append((own + other.astype(F32)).astype(BF16))

    groups = []
    for c, y in enumerate(solved):
        pieces = gather(y)
        if c:
            own, other = partials(*cpl, pieces[:-1], other_type=F32)
            place = len(pieces) - 1
            other = last_part(cpl[1], pieces[-1], other, place, BF16)
            own = last_part(cpl[0], pieces[-1], own, place, F32)
        else:
            own, other = partials(*cpl, pieces)
        other = partner(other)
        group = list(split(own, other, leaves))
        for d in range(1, leaves):
            group[d] = lax.ppermute(group[d], "leaf", [(j, j ^ d) for j in range(leaves)])
        if not c:
            group = [sum((g.astype(F32) for g in group[1:]), group[0])]
        groups.append(group)

    solution = join(*solved, leaves)
    out = finish(ancestor_rhs, groups)
    return (solution[None], out)


def solution(mesh):
    return jax.shard_map(
        on_device,
        mesh=mesh,
        in_specs=(
            P("leaf", "row", None),
            P("leaf", "row", None),
            P("leaf", "row", None),
            P("leaf", "row"),
            P("row", "leaf"),
        ),
        out_specs=(P("leaf", "row", None), P("row", "leaf")),
        check_vma=False,
    )
```
